32 devices in a mesh: seq: 8 (over y, x, core), head: 4 (over z).
Axes of the slice: x: 2, y: 2, z: 4, core: 2. Of those that a mesh axis runs over, the one named last changes fastest.
Arguments:
- queries: float32 [1024, 2048], P('seq', 'head'), may hold values from -24 to 24
- keys: float32 [1024, 512], P('seq', 'head'), may hold values from -24 to 24
- values: float32 [1024, 512], P('seq', 'head'), may hold values from -6 to 6
- grad_out: float32 [1024, 2048], P('seq', 'head'), may hold values from -6 to 6
- out_weight: float32 [2048, 2048], P('head'), may hold values from -0.125 to 0.125
Outputs:
- grad_q: float32 [1024, 2048], P('seq', 'head')
- grad_k: float32 [1024, 512], P('seq', 'head')
- grad_v: float32 [1024, 512], P('seq', 'head')
- grad_wo: float32 [2048, 2048], P('head', 'seq')
The draws below stay inside these ranges and needn't reach their ends.
All inputs are finite; a program needn't handle non-finite values.
Results may differ from the reference program's by a relative error of at most 0.0003.
Values sent between devices are 32-bit elements; how exact they have to be, the bound alone decides.
No kernel may reach another device: no remote copies, remote signals or barrier semaphores. Data moves between devices by JAX's collectives and lax.ppermute only.
A program may use at most 128 MiB of HBM per device.

```python
import math
import jax
import jax.numpy as jnp
from jax import lax

D = 2048
HD = 128
KV_HEADS = 4
HEADS = 16
GROUP = 4
SEQ = 1024


def paired_draw(base_key):
    draw_query, draw_keyrows = jax.random.split(jax.random.fold_in(base_key, 7), 2)
    queries = jnp.clip(jax.random.normal(draw_query, (SEQ, HEADS * HD), jnp.float32), -6.0, 6.0)
    keys_all = jnp.clip(jax.random.normal(draw_keyrows, (SEQ, KV_HEADS * HD), jnp.float32), -6.0, 6.0)
    return (queries, keys_all)


def draw_queries(key, part):
    return paired_draw(key)[0]


def draw_keys(key, part):
    return paired_draw(key)[1]


def with_spikes(array, stream_key, source, target, shards_of, factor):
    owner, partner = [(jnp.arange(array.shape[axis_at]) // (array.shape[axis_at] // shards_of)).reshape([-1 if axis == axis_at else 1 for axis in range(array.ndim)]) for axis_at in (source, target)]
    chosen = jax.random.permutation(stream_key, shards_of)[partner]
    strong = (owner == chosen) | (owner == (partner + shards_of // 2) % shards_of)
    return jnp.where(strong, factor * array, array)


def levels(stream_key, dims, pieces, smallest, high):
    def one(axis_at, parts):
        heights = jax.random.uniform(jax.random.fold_in(jax.random.fold_in(stream_key, 6), axis_at), (parts,), jnp.float32, smallest / len(pieces), high / len(pieces))
        return jnp.repeat(jnp.exp(heights), dims[axis_at] // parts).reshape((-1,) + (1,) * (len(dims) - axis_at - 1))

    loudness = one(*pieces[0])
    for cut in pieces[1:]:
        loudness = loudness * one(*cut)
    return loudness


def noise(rng, shape, spread, reach, cuts=(), kind=jnp.bfloat16):
    entries = jax.random.normal(rng, shape, jnp.float32) * spread
    if len(cuts) > 0:
        entries = levels(rng, shape, cuts, -0.22, 0.18) * entries
    return jnp.clip(entries, min=-reach, max=reach).astype(kind)


def heavy_noise(stream_key, shape, spread, bound, cuts, heavy, held_as=jnp.bfloat16):
    values = spread * jax.random.normal(stream_key, shape, jnp.float32)
    if cuts:
        values = values * levels(stream_key, shape, cuts, -0.22, 0.18)
    return jnp.clip(with_spikes(values, jax.random.fold_in(stream_key, 3), *heavy), -bound, bound).astype(held_as)


def setup_inputs(seed: int = 0) -> dict:
    streams_of = jax.random.split(jax.random.key(seed), 6)
    queries = draw_queries(jax.random.fold_in(streams_of[5], 71), 0)
    keys = draw_keys(jax.random.fold_in(streams_of[5], 71), 0)
    values = noise(streams_of[2], (SEQ, KV_HEADS * HD), 1.0, 6.0, ((0, 8), (1, 4)), jnp.float32)
    grad_out = heavy_noise(streams_of[3], (SEQ, D), 1.0, 6.0, ((0, 8), (1, 4)), (0, 1, 8, 2.0), jnp.float32)
    out_weight = noise(streams_of[4], (HEADS * HD, D), (HEADS * HD) ** -0.5, 0.125, ((0, 4),), jnp.float32)
    return {"queries": queries, "keys": keys, "values": values, "grad_out": grad_out, "out_weight": out_weight}


HIGHEST = lax.Precision.HIGHEST

def reference(queries, keys, values, grad_out, out_weight):
    seq_len = queries.shape[0]
    score_scale = 1.0 / math.sqrt(HD)
    q_heads = queries.reshape(seq_len, HEADS, HD).transpose(1, 0, 2)
    k_heads = keys.reshape(seq_len, KV_HEADS, HD).transpose(1, 0, 2)
    v_heads = values.reshape(seq_len, KV_HEADS, HD).transpose(1, 0, 2)
    d_attn = jnp.dot(grad_out, out_weight.T, precision=HIGHEST)
    d_heads = d_attn.reshape(seq_len, HEADS, HD).transpose(1, 0, 2)
    position = jnp.arange(seq_len, dtype=jnp.int32)
    visible = position[None, :] <= position[:, None]

    def one_head(head_index):
        query_now = lax.dynamic_index_in_dim(q_heads, head_index, 0, keepdims=False)
        grad_now = lax.dynamic_index_in_dim(d_heads, head_index, 0, keepdims=False)
        key_now = lax.dynamic_index_in_dim(k_heads, head_index // GROUP, 0, keepdims=False)
        value_now = lax.dynamic_index_in_dim(v_heads, head_index // GROUP, 0, keepdims=False)
        score = jnp.dot(query_now, key_now.T, precision=HIGHEST) * score_scale
        score = jnp.where(visible, score, -jnp.inf)
        log_norm = jax.nn.logsumexp(score, axis=1)
        prob_full = jnp.where(visible, jnp.exp(score - log_norm[:, None]), 0.0)
        outputs = jnp.dot(prob_full, value_now, precision=HIGHEST)
        delta_rows = lax.optimization_barrier(jnp.sum(outputs * grad_now, axis=1))
        grad_prob = jnp.dot(grad_now, value_now.T, precision=HIGHEST)
        grad_score = prob_full * (grad_prob - delta_rows[:, None]) * score_scale
        grad_query = jnp.dot(grad_score, key_now, precision=HIGHEST)
        grad_key = jnp.dot(grad_score.T, query_now, precision=HIGHEST)
        grad_value = jnp.dot(prob_full.T, grad_now, precision=HIGHEST)
        return (outputs, grad_query, grad_key, grad_value)
    outputs, grad_query, grad_key, grad_value = lax.map(one_head, jnp.arange(HEADS, dtype=jnp.int32))
    attn = outputs.transpose(1, 0, 2).reshape(seq_len, HEADS * HD)
    grad_q = grad_query.transpose(1, 0, 2).reshape(seq_len, HEADS * HD)
    grad_k = grad_key.reshape(KV_HEADS, GROUP, seq_len, HD).sum(axis=1).transpose(1, 0, 2).reshape(seq_len, KV_HEADS * HD)
    grad_v = grad_value.reshape(KV_HEADS, GROUP, seq_len, HD).sum(axis=1).transpose(1, 0, 2).reshape(seq_len, KV_HEADS * HD)
    grad_wo = jnp.dot(attn.T, grad_out, precision=HIGHEST)
    return (grad_q, grad_k, grad_v, grad_wo)
```

```python
import functools
import math

import jax
import jax.numpy as jnp
from jax import lax
from jax.experimental import pallas as pl
from jax.experimental.pallas import tpu as pltpu
from jax.sharding import PartitionSpec as P

HD = 128
GROUP = 4
CORES = 2
MASKED = -1e30
F32 = jnp.float32
BF16 = jnp.bfloat16

NN = (((1,), (0,)), ((), ()))
NT = (((1,), (1,)), ((), ()))


def mm(a, b, dims=NN):
    return lax.dot_general(a, b, dims, preferred_element_type=F32)


def two(x):
    hi = x.astype(BF16)
    return hi, (x - hi.astype(F32)).astype(BF16)


def three(x):
    first = x.astype(BF16)
    rest = x - first.astype(F32)
    second = rest.astype(BF16)
    return first, second, (rest - second.astype(F32)).astype(BF16)


def params():
    return pltpu.CompilerParams(vmem_limit_bytes=48 * 1024 * 1024)


def load_blocks(refs, dst, column):
    row = 0
    for ref in refs:
        count = ref.shape[0]
        dst[row : row + count, :] = ref[:, column : column + HD]
        row += count


def forward_kernel(score_scale, q_ref, *refs):
    pieces = refs[:-6]
    attn_ref, exp_ref, inv_ref, keys, values, score = refs[-6:]
    tokens = q_ref.shape[0]
    rows = GROUP * tokens
    total = keys.shape[0]
    blocks = total // tokens
    chips = blocks // CORES
    me = lax.axis_index("seq")
    load_blocks(pieces, keys, 0)
    load_blocks(pieces, values, HD)
    q = jnp.concatenate([q_ref[:, g * HD : (g + 1) * HD] for g in range(GROUP)], axis=0)
    q1, q2, q3 = three(q)
    q11 = jnp.concatenate([q1, q1], axis=1)
    q22 = jnp.concatenate([q2, q2], axis=1)
    q13 = jnp.concatenate([q1, q3], axis=1)
    key_row = lax.broadcasted_iota(jnp.int32, (tokens, rows), 0)
    query_row = lax.broadcasted_iota(jnp.int32, (tokens, rows), 1) % tokens
    offset = key_row - query_row

    def scores(b, top):
        own = (b // chips) ^ (me % CORES)
        block = ((me // CORES) ^ (b % chips)) * CORES + own
        at = pl.ds(pl.multiple_of(b * tokens, tokens), tokens)
        k1, k2, k3 = three(keys[at, :])
        k12 = jnp.concatenate([k1, k2], axis=1)
        k31 = jnp.concatenate([k3, k1], axis=1)
        s = mm(k31, q13, NT) + mm(k12, q22, NT) + mm(k12, q11, NT)
        s = jnp.where(offset <= (me - block) * tokens, s * score_scale, MASKED)
        score[at, :] = s
        return jnp.maximum(top, jnp.max(s, axis=0, keepdims=True))

    top = lax.fori_loop(0, blocks, scores, jnp.full((1, rows), MASKED, F32), unroll=2)

    def weigh(b, state):
        norm, acc = state
        at = pl.ds(pl.multiple_of(b * tokens, tokens), tokens)
        e = jnp.exp(score[at, :] - top)
        exp_ref[at, :] = e
        eh, el = two(e)
        vh, vl = two(values[at, :].T)
        both = mm(jnp.concatenate([vh, vl], axis=0), eh)
        acc = acc + (both[:HD] + both[HD:] + mm(vh, el))
        return norm + jnp.sum(e, axis=0, keepdims=True), acc

    norm, acc = lax.fori_loop(
        0, blocks, weigh, (jnp.zeros((1, rows), F32), jnp.zeros((HD, rows), F32)), unroll=2
    )
    inv = 1.0 / norm
    inv_ref[...] = jnp.broadcast_to(inv, inv_ref.shape)
    out = acc * inv
    for g in range(GROUP):
        attn_ref[g * HD : (g + 1) * HD, :] = out[:, g * tokens : (g + 1) * tokens]


def forward(q, pieces, total, score_scale):
    tokens = q.shape[0]
    rows = GROUP * tokens
    return pl.pallas_call(
        functools.partial(forward_kernel, score_scale),
        out_shape=(
            jax.ShapeDtypeStruct((GROUP * HD, tokens), F32),
            jax.ShapeDtypeStruct((total, rows), F32),
            jax.ShapeDtypeStruct((8, rows), F32),
        ),
        scratch_shapes=[
            pltpu.VMEM((total, HD), F32),
            pltpu.VMEM((total, HD), F32),
            pltpu.VMEM((total, rows), F32),
        ],
        compiler_params=params(),
        name="attn_fwd",
    )(q, *pieces)


def backward_kernel(score_scale, q_ref, d_ref, exp_ref, inv_ref, *refs):
    pieces = refs[:-6]
    dq_ref, keep_ref, send_ref, keys, values, dp_ref = refs[-6:]
    tokens = q_ref.shape[0]
    rows = GROUP * tokens
    total = keys.shape[0]
    blocks = total // tokens
    load_blocks(pieces, keys, 0)
    load_blocks(pieces, values, HD)
    q = jnp.concatenate([q_ref[:, g * HD : (g + 1) * HD] for g in range(GROUP)], axis=0)
    qh, ql = two(q)
    qhl = jnp.concatenate([qh, ql], axis=1)
    d = jnp.concatenate([d_ref[g * HD : (g + 1) * HD, :] for g in range(GROUP)], axis=1)
    dh, dl = two(d)
    dhh = jnp.concatenate([dh, dh], axis=0)
    dhl = jnp.concatenate([dh, dl], axis=0)
    inv = inv_ref[0:1, :]

    def probs(b, delta):
        at = pl.ds(pl.multiple_of(b * tokens, tokens), tokens)
        vh, vl = two(values[at, :])
        dp = mm(vh, dl) + mm(jnp.concatenate([vh, vl], axis=1), dhh)
        dp_ref[at, :] = dp
        return delta + jnp.sum(exp_ref[at, :] * dp, axis=0, keepdims=True)

    delta = lax.fori_loop(0, blocks, probs, jnp.zeros((1, rows), F32), unroll=2) * inv

    def grads(b, acc, out_ref, first):
        at = pl.ds(pl.multiple_of(b * tokens, tokens), tokens)
        to = pl.ds(pl.multiple_of((b - first) * tokens, tokens), tokens)
        p = exp_ref[at, :] * inv
        ds = p * (dp_ref[at, :] - delta) * score_scale
        ph, plo = two(p)
        sh, sl = two(ds)
        kh, kl = two(keys[at, :].T)
        both = mm(jnp.concatenate([kh, kl], axis=0), sh)
        acc = acc + (both[:HD] + both[HD:] + mm(kh, sl))
        dk = mm(sh, qhl)
        out_ref[to, 0:HD] = dk[:, :HD] + dk[:, HD:] + mm(sl, qh)
        dv = mm(ph, dhl, NT)
        out_ref[to, HD : 2 * HD] = dv[:, :HD] + dv[:, HD:] + mm(plo, dh, NT)
        return acc

    acc = jnp.zeros((HD, rows), F32)
    mid = blocks // CORES
    acc = lax.fori_loop(mid, blocks, lambda b, a: grads(b, a, send_ref, mid), acc, unroll=2)
    acc = lax.fori_loop(0, mid, lambda b, a: grads(b, a, keep_ref, 0), acc, unroll=2)
    for g in range(GROUP):
        dq_ref[:, g * HD : (g + 1) * HD] = acc[:, g * tokens : (g + 1) * tokens].T


def backward(q, d_attn, weights, inv, pieces, score_scale):
    tokens = q.shape[0]
    total, rows = weights.shape
    half = total // CORES
    return pl.pallas_call(
        functools.partial(backward_kernel, score_scale),
        out_shape=(
            jax.ShapeDtypeStruct(q.shape, F32),
            jax.ShapeDtypeStruct((half, 2 * HD), F32),
            jax.ShapeDtypeStruct((half, 2 * HD), F32),
        ),
        scratch_shapes=[
            pltpu.VMEM((total, HD), F32),
            pltpu.VMEM((total, HD), F32),
            pltpu.VMEM((total, rows), F32),
        ],
        compiler_params=params(),
        name="attn_bwd",
    )(q, d_attn, weights, inv, *pieces)


def project_kernel(side, width, w_ref, *refs):
    heads = lax.axis_size("head")
    pieces = refs[: 2 * heads]
    d_ref = refs[2 * heads]
    outs = refs[2 * heads + 1 : -1]
    full = refs[-1]
    tokens, columns = full.shape
    part = columns // heads
    upper = tokens // 2
    me = lax.axis_index("head")
    for i, (offset, _) in enumerate(ring_pieces(heads)):
        at = pl.ds(pl.multiple_of(((me + offset + heads) % heads) * part, part), part)
        full[:upper, at] = pieces[2 * i][...]
        full[upper:, at] = pieces[2 * i + 1][...]
    g_hi, g_lo = two(full[...])
    g_both = jnp.concatenate([g_hi, g_lo], axis=0)
    step = 128
    for row in range(0, w_ref.shape[0], step):
        w_hi, w_lo = two(w_ref[row : row + step, :])
        both = mm(w_hi, g_both, NT)
        d_ref[row : row + step, :] = both[:, :tokens] + both[:, tokens:] + mm(w_lo, g_hi, NT)
    if outs:
        seq = lax.axis_index("seq")
        core = seq % CORES
        chip = seq // CORES
        x, y = chip % side, chip // side
        for out, (other_core, j) in zip(outs, column_sets(side)):
            kind = core ^ other_core
            fixed = jnp.where(kind == 0, x, y) ^ j
            moving = jnp.where(kind == 0, y, x)
            for t in range(side):
                i = moving ^ t
                index = jnp.where(kind == 0, i * side + fixed, fixed * side + i)
                at = pl.multiple_of((index * CORES + kind) * width, width)
                out[:, t * width : (t + 1) * width] = full[:, pl.ds(at, width)]


def ring_pieces(heads):
    found = [(0, 0)]
    for step in range(1, heads // 2 + 1):
        found.append((-step, 1))
        if 2 * step != heads:
            found.append((step, -1))
    return found


def column_sets(side):
    sets = [(0, 0)]
    for j in range(side):
        if j:
            sets.append((0, j))
        sets.append((1, j))
    return sets


def project(out_weight, pieces, side, width):
    tokens = 2 * pieces[0].shape[0]
    rows, columns = out_weight.shape
    shapes = [jax.ShapeDtypeStruct((rows, tokens), F32)]
    if side:
        shapes += [jax.ShapeDtypeStruct((tokens, side * width), F32)] * len(column_sets(side))
    return pl.pallas_call(
        functools.partial(project_kernel, side, width),
        out_shape=tuple(shapes),
        scratch_shapes=[pltpu.VMEM((tokens, columns), F32)],
        compiler_params=params(),
        name="project",
    )(out_weight, *pieces)


def weight_kernel(count, *refs):
    attn = refs[:count]
    grad = refs[count : 2 * count]
    outs = refs[2 * count :]
    width = outs[0].shape[1]
    a_hi, a_lo = two(jnp.concatenate([ref[...] for ref in attn], axis=1))
    for t, out in enumerate(outs):
        cut = slice(t * width, (t + 1) * width)
        g_hi, g_lo = two(jnp.concatenate([ref[:, cut] for ref in grad], axis=0))
        out[...] = mm(a_hi, g_lo) + mm(a_lo, g_hi) + mm(a_hi, g_hi)


def weight_grad(attn, grad, side, width):
    rows = attn[0].shape[0]
    return pl.pallas_call(
        functools.partial(weight_kernel, len(attn)),
        out_shape=(jax.ShapeDtypeStruct((rows, width), F32),) * side,
        compiler_params=params(),
        name="weight_grad",
    )(*attn, *grad)


def body(queries, keys, values, grad_out, out_weight):
    tokens = queries.shape[0]
    seq = lax.axis_size("seq")
    heads = lax.axis_size("head")
    chips = seq // CORES
    total = seq * tokens
    width = out_weight.shape[1] // seq
    score_scale = 1.0 / math.sqrt(HD)
    side = math.isqrt(chips)
    exchange = side * side == chips and width % 128 == 0

    def swap(block):
        return lax.ppermute(block, "seq", [(i, i ^ 1) for i in range(seq)])

    def to_chip(block, j):
        return lax.ppermute(block, "seq", [(i, i ^ (CORES * j)) for i in range(seq)])

    def along(block, step):
        return lax.ppermute(block, "head", [(i, (i + step) % heads) for i in range(heads)])

    own = jnp.concatenate([keys, values], axis=1)
    same = [own] + [to_chip(own, j) for j in range(1, chips)]

    upper = tokens // 2
    top, bottom = grad_out[:upper], grad_out[upper:]
    grad_pieces = [top, bottom]
    right, left = (top, bottom), (top, bottom)
    for step in range(1, heads // 2 + 1):
        if 2 * step == heads:
            grad_pieces += [along(right[0], 1), along(left[1], -1)]
        else:
            right = tuple(along(piece, 1) for piece in right)
            left = tuple(along(piece, -1) for piece in left)
            grad_pieces += [*right, *left]

    pieces = same + [swap(jnp.concatenate(same, axis=0))]
    attn, weights, inv = forward(queries, pieces, total, score_scale)
    d_attn, *column = project(out_weight, grad_pieces, side if exchange else 0, width)

    if exchange:

        def routes(cross, j):
            found = []
            for i in range(seq):
                core, chip = i % CORES, i // CORES
                kind = core ^ cross
                x, y = chip % side, chip // side
                if kind == 0:
                    x ^= j
                else:
                    y ^= j
                found.append((i, (y * side + x) * CORES + kind))
            return found

        sets = column_sets(side)
        moved_grad = [column[0]] + [
            lax.ppermute(c, "seq", routes(*s)) for s, c in zip(sets[1:], column[1:])
        ]
        moved_attn = [attn] + [lax.ppermute(attn, "seq", routes(*s)) for s in sets[1:]]
        partial = weight_grad(moved_attn, moved_grad, side, width)

        def final_routes(t):
            found = []
            for i in range(seq):
                core, chip = i % CORES, i // CORES
                x, y = chip % side, chip // side
                if core == 0:
                    y ^= t
                else:
                    x ^= t
                found.append((i, (y * side + x) * CORES + core))
            return found

        grad_wo = partial[0]
        for t in range(1, side):
            grad_wo = grad_wo + lax.ppermute(partial[t], "seq", final_routes(t))
    else:
        grad_full = lax.all_gather(grad_out, "head", axis=1, tiled=True)
        grad_wo = lax.psum_scatter(
            jnp.dot(grad_full.T, attn.T, precision=lax.Precision.HIGHEST),
            "seq",
            scatter_dimension=0,
            tiled=True,
        ).T

    grad_q, keep, send = backward(queries, d_attn, weights, inv, pieces, score_scale)
    summed = (keep + swap(send)).reshape(chips, tokens, 2 * HD)
    grad_kv = summed[0]
    for j in range(1, chips):
        grad_kv = grad_kv + to_chip(summed[j], j)
    return (grad_q, grad_kv[:, :HD], grad_kv[:, HD:], grad_wo)


def solution(mesh):
    in_specs = (
        P("seq", "head"),
        P("seq", "head"),
        P("seq", "head"),
        P("seq", "head"),
        P("head", None),
    )
    out_specs = (P("seq", "head"), P("seq", "head"), P("seq", "head"), P("head", "seq"))
    return jax.shard_map(body, mesh=mesh, in_specs=in_specs, out_specs=out_specs, check_vma=False)
```

```python
import functools
import math

import jax
import jax.numpy as jnp
from jax import lax
from jax.experimental import pallas as pl
from jax.experimental.pallas import tpu as pltpu
from jax.sharding import PartitionSpec as P

HD = 128
GROUP = 4
CORES = 2
MASKED = -1e30
F32 = jnp.float32
BF16 = jnp.bfloat16

NN = (((1,), (0,)), ((), ()))
NT = (((1,), (1,)), ((), ()))


def mm(a, b, dims=NN):
    return lax.dot_general(a, b, dims, preferred_element_type=F32)


def two(x):
    hi = x.astype(BF16)
    return hi, (x - hi.astype(F32)).astype(BF16)


def three(x):
    first = x.astype(BF16)
    rest = x - first.astype(F32)
    second = rest.astype(BF16)
    return first, second, (rest - second.astype(F32)).astype(BF16)


def cost(flops, size):
    return pl.CostEstimate(flops=flops, transcendentals=0, bytes_accessed=size)


def params():
    return pltpu.CompilerParams(vmem_limit_bytes=48 * 1024 * 1024)


def load_blocks(refs, dst, column):
    row = 0
    for ref in refs:
        count = ref.shape[0]
        dst[row : row + count, :] = ref[:, column : column + HD]
        row += count


def forward_kernel(score_scale, q_ref, *refs):
    pieces = refs[:-6]
    attn_ref, exp_ref, inv_ref, keys, values, score = refs[-6:]
    tokens = q_ref.shape[0]
    rows = GROUP * tokens
    total = keys.shape[0]
    blocks = total // tokens
    chips = blocks // CORES
    me = lax.axis_index("seq")
    load_blocks(pieces, keys, 0)
    load_blocks(pieces, values, HD)
    q1, q2, q3 = three(stacked_queries(q_ref))
    q11 = jnp.concatenate([q1, q1], axis=1)
    q22 = jnp.concatenate([q2, q2], axis=1)
    q13 = jnp.concatenate([q1, q3], axis=1)
    key_row = lax.broadcasted_iota(jnp.int32, (tokens, rows), 0)
    query_row = lax.broadcasted_iota(jnp.int32, (tokens, rows), 1) % tokens
    offset = key_row - query_row

    def scores(b, top):
        own = (b // chips) ^ (me % CORES)
        block = ((me // CORES) ^ (b % chips)) * CORES + own
        at = pl.ds(pl.multiple_of(b * tokens, tokens), tokens)
        k1, k2, k3 = three(keys[at, :])
        k12 = jnp.concatenate([k1, k2], axis=1)
        k31 = jnp.concatenate([k3, k1], axis=1)
        s = mm(k31, q13, NT) + mm(k12, q22, NT) + mm(k12, q11, NT)
        s = jnp.where(offset <= (me - block) * tokens, s * score_scale, MASKED)
        score[at, :] = s
        return jnp.maximum(top, jnp.max(s, axis=0, keepdims=True))

    top = lax.fori_loop(0, blocks, scores, jnp.full((1, rows), MASKED, F32), unroll=2)

    def weigh(b, state):
        norm, acc = state
        at = pl.ds(pl.multiple_of(b * tokens, tokens), tokens)
        e = jnp.exp(score[at, :] - top)
        exp_ref[at, :] = e
        eh, el = two(e)
        vh, vl = two(values[at, :].T)
        both = mm(jnp.concatenate([vh, vl], axis=0), eh)
        acc = acc + (both[:HD] + both[HD:] + mm(vh, el))
        return norm + jnp.sum(e, axis=0, keepdims=True), acc

    norm, acc = lax.fori_loop(
        0, blocks, weigh, (jnp.zeros((1, rows), F32), jnp.zeros((HD, rows), F32)), unroll=2
    )
    inv = 1.0 / norm
    inv_ref[...] = jnp.broadcast_to(inv, inv_ref.shape)
    out = acc * inv
    for g in range(GROUP):
        attn_ref[g * HD : (g + 1) * HD, :] = out[:, g * tokens : (g + 1) * tokens]


def forward(q, pieces, total, score_scale):
    tokens = q.shape[0]
    rows = GROUP * tokens
    return pl.pallas_call(
        functools.partial(forward_kernel, score_scale),
        out_shape=(
            jax.ShapeDtypeStruct((GROUP * HD, tokens), F32),
            jax.ShapeDtypeStruct((total, rows), F32),
            jax.ShapeDtypeStruct((8, rows), F32),
        ),
        scratch_shapes=[
            pltpu.VMEM((total, HD), F32),
            pltpu.VMEM((total, HD), F32),
            pltpu.VMEM((total, rows), F32),
        ],
        compiler_params=params(),
        cost_estimate=cost(36 * total * rows * HD, 8 * total * rows),
        name="attn_fwd",
    )(q, *pieces)


def stacked_queries(q_ref):
    return jnp.concatenate([q_ref[:, g * HD : (g + 1) * HD] for g in range(GROUP)], axis=0)


def stacked_grads(d_ref):
    return jnp.concatenate([d_ref[g * HD : (g + 1) * HD, :] for g in range(GROUP)], axis=1)


def key_grads(score_scale, first, q, d, exp_ref, inv, dp_ref, delta, keys, out_ref, acc):
    rows = q.shape[0]
    tokens = rows // GROUP
    qh, ql = two(q)
    qhl = jnp.concatenate([qh, ql], axis=1)
    dh, dl = two(d)
    dhl = jnp.concatenate([dh, dl], axis=0)

    def grads(b, acc):
        to = pl.ds(pl.multiple_of(b * tokens, tokens), tokens)
        at = pl.ds(pl.multiple_of(first + b * tokens, tokens), tokens)
        p = exp_ref[at, :] * inv
        ds = p * (dp_ref[at, :] - delta) * score_scale
        ph, plo = two(p)
        sh, sl = two(ds)
        kh, kl = two(keys[to, :].T)
        both = mm(jnp.concatenate([kh, kl], axis=0), sh)
        acc = acc + (both[:HD] + both[HD:] + mm(kh, sl))
        dk = mm(sh, qhl)
        out_ref[to, 0:HD] = dk[:, :HD] + dk[:, HD:] + mm(sl, qh)
        dv = mm(ph, dhl, NT)
        out_ref[to, HD : 2 * HD] = dv[:, :HD] + dv[:, HD:] + mm(plo, dh, NT)
        return acc

    return lax.fori_loop(0, out_ref.shape[0] // tokens, grads, acc, unroll=2)


def backward_far_kernel(score_scale, q_ref, d_ref, exp_ref, inv_ref, *refs):
    pieces = refs[:-6]
    acc_ref, dp_ref, delta_ref, send_ref, keys, values = refs[-6:]
    tokens = q_ref.shape[0]
    rows = GROUP * tokens
    total = values.shape[0]
    load_blocks(pieces[-1:], keys, 0)
    load_blocks(pieces, values, HD)
    d = stacked_grads(d_ref)
    dh, dl = two(d)
    dhh = jnp.concatenate([dh, dh], axis=0)
    inv = inv_ref[0:1, :]

    def probs(b, delta):
        at = pl.ds(pl.multiple_of(b * tokens, tokens), tokens)
        vh, vl = two(values[at, :])
        dp = mm(vh, dl) + mm(jnp.concatenate([vh, vl], axis=1), dhh)
        dp_ref[at, :] = dp
        return delta + jnp.sum(exp_ref[at, :] * dp, axis=0, keepdims=True)

    delta = lax.fori_loop(0, total // tokens, probs, jnp.zeros((1, rows), F32), unroll=2) * inv
    delta_ref[...] = jnp.broadcast_to(delta, delta_ref.shape)
    acc_ref[...] = key_grads(
        score_scale,
        total - send_ref.shape[0],
        stacked_queries(q_ref),
        d,
        exp_ref,
        inv,
        dp_ref,
        delta,
        keys,
        send_ref,
        jnp.zeros((HD, rows), F32),
    )


def backward_near_kernel(
    score_scale, q_ref, d_ref, exp_ref, inv_ref, acc_ref, dp_ref, delta_ref, *refs
):
    pieces = refs[:-3]
    dq_ref, keep_ref, keys = refs[-3:]
    tokens = q_ref.shape[0]
    load_blocks(pieces, keys, 0)
    acc = key_grads(
        score_scale,
        0,
        stacked_queries(q_ref),
        stacked_grads(d_ref),
        exp_ref,
        inv_ref[0:1, :],
        dp_ref,
        delta_ref[0:1, :],
        keys,
        keep_ref,
        acc_ref[...],
    )
    for g in range(GROUP):
        dq_ref[:, g * HD : (g + 1) * HD] = acc[:, g * tokens : (g + 1) * tokens].T


def backward_far(q, d_attn, weights, inv, pieces, score_scale):
    total, rows = weights.shape
    half = total // CORES
    return pl.pallas_call(
        functools.partial(backward_far_kernel, score_scale),
        out_shape=(
            jax.ShapeDtypeStruct((HD, rows), F32),
            jax.ShapeDtypeStruct((total, rows), F32),
            jax.ShapeDtypeStruct((8, rows), F32),
            jax.ShapeDtypeStruct((half, 2 * HD), F32),
        ),
        scratch_shapes=[pltpu.VMEM((half, HD), F32), pltpu.VMEM((total, HD), F32)],
        compiler_params=params(),
        cost_estimate=cost(24 * total * rows * HD, 8 * total * rows),
        name="attn_bwd_far",
    )(q, d_attn, weights, inv, *pieces)


def backward_near(q, d_attn, weights, inv, carried, pieces, score_scale):
    total, rows = weights.shape
    half = total // CORES
    return pl.pallas_call(
        functools.partial(backward_near_kernel, score_scale),
        out_shape=(
            jax.ShapeDtypeStruct(q.shape, F32),
            jax.ShapeDtypeStruct((half, 2 * HD), F32),
        ),
        scratch_shapes=[pltpu.VMEM((half, HD), F32)],
        compiler_params=params(),
        cost_estimate=cost(18 * total * rows * HD, 8 * total * rows),
        name="attn_bwd_near",
    )(q, d_attn, weights, inv, *carried, *pieces)


def project_kernel(side, width, w_ref, *refs):
    heads = lax.axis_size("head")
    blocks = ring_pieces(heads)
    pieces = refs[: len(blocks)]
    d_ref = refs[len(blocks)]
    outs = refs[len(blocks) + 1 : -1]
    full = refs[-1]
    tokens, columns = full.shape
    part = columns // heads
    me = lax.axis_index("head")
    for piece, (offset, first, count) in zip(pieces, blocks):
        at = pl.ds(pl.multiple_of(((me + offset) % heads) * part, part), part)
        first, count = first * tokens // 2, count * tokens // 2
        full[first : first + count, at] = piece[...]
    g_hi, g_lo = two(full[...])
    g_both = jnp.concatenate([g_hi, g_lo], axis=0)
    step = 128
    for row in range(0, w_ref.shape[0], step):
        w_hi, w_lo = two(w_ref[row : row + step, :])
        both = mm(w_hi, g_both, NT)
        d_ref[row : row + step, :] = both[:, :tokens] + both[:, tokens:] + mm(w_lo, g_hi, NT)
    if outs:
        seq = lax.axis_index("seq")
        core = seq % CORES
        chip = seq // CORES
        x, y = chip % side, chip // side
        for out, (other_core, j) in zip(outs, column_sets(side)):
            kind = core ^ other_core
            fixed = jnp.where(kind == 0, x, y) ^ j
            moving = jnp.where(kind == 0, y, x)
            for t in range(side):
                i = moving ^ t
                index = jnp.where(kind == 0, i * side + fixed, fixed * side + i)
                at = pl.multiple_of((index * CORES + kind) * width, width)
                out[:, t * width : (t + 1) * width] = full[:, pl.ds(at, width)]


def ring_pieces(heads):
    found = [(0, 0, 2)]
    for step in range(1, heads // 2 + 1):
        if 2 * step == heads:
            found += [(heads - step, 0, 1), (step, 1, 1)]
        else:
            found += [(heads - step, 0, 2), (step, 0, 2)]
    return found


def column_sets(side):
    sets = [(0, 0)]
    for j in range(side):
        if j:
            sets.append((0, j))
        sets.append((1, j))
    return sets


def project(out_weight, pieces, side, width):
    tokens = pieces[0].shape[0]
    rows, columns = out_weight.shape
    shapes = [jax.ShapeDtypeStruct((rows, tokens), F32)]
    if side:
        shapes += [jax.ShapeDtypeStruct((tokens, side * width), F32)] * len(column_sets(side))
    return pl.pallas_call(
        functools.partial(project_kernel, side, width),
        out_shape=tuple(shapes),
        scratch_shapes=[pltpu.VMEM((tokens, columns), F32)],
        compiler_params=params(),
        cost_estimate=cost(24 * tokens * rows * columns, 4 * rows * columns),
        name="project",
    )(out_weight, *pieces)


def weight_kernel(count, *refs):
    attn = refs[:count]
    grad = refs[count : 2 * count]
    outs = refs[2 * count :]
    width = outs[0].shape[1]
    a_hi, a_lo = two(jnp.concatenate([ref[...] for ref in attn], axis=1))
    for t, out in enumerate(outs):
        cut = slice(t * width, (t + 1) * width)
        g_hi, g_lo = two(jnp.concatenate([ref[:, cut] for ref in grad], axis=0))
        out[...] = mm(a_hi, g_lo) + mm(a_lo, g_hi) + mm(a_hi, g_hi)


def weight_grad(attn, grad, side, width):
    rows = attn[0].shape[0]
    return pl.pallas_call(
        functools.partial(weight_kernel, len(attn)),
        out_shape=(jax.ShapeDtypeStruct((rows, width), F32),) * side,
        compiler_params=params(),
        cost_estimate=cost(2 * rows * rows * width * side, 8 * rows * width * side),
        name="weight_grad",
    )(*attn, *grad)


def body(queries, keys, values, grad_out, out_weight):
    tokens = queries.shape[0]
    seq = lax.axis_size("seq")
    heads = lax.axis_size("head")
    chips = seq // CORES
    total = seq * tokens
    width = out_weight.shape[1] // seq
    score_scale = 1.0 / math.sqrt(HD)
    side = math.isqrt(chips)
    exchange = side * side == chips and width % 128 == 0

    def swap(block):
        return lax.ppermute(block, "seq", [(i, i ^ 1) for i in range(seq)])

    def to_chip(block, j):
        return lax.ppermute(block, "seq", [(i, i ^ (CORES * j)) for i in range(seq)])

    def along(block, step):
        return lax.ppermute(block, "head", [(i, (i + step) % heads) for i in range(heads)])

    upper = tokens // 2
    grad_pieces = [grad_out]
    right = left = grad_out
    for step in range(1, heads // 2 + 1):
        if 2 * step == heads:
            right = along(right[:upper], 1)
            left = along(left[upper:], -1)
            grad_pieces += [right, left]
        else:
            right = along(right, 1)
            left = along(left, -1)
            grad_pieces += [right, left]

    own = jnp.concatenate([keys, values], axis=1)
    same = [own]
    for j in range(1, chips):
        same.append(to_chip(own, j))
    pieces = same + [swap(jnp.concatenate(same, axis=0))]

    attn, weights, inv = forward(queries, pieces, total, score_scale)
    d_attn, *column = project(out_weight, grad_pieces, side if exchange else 0, width)

    if exchange:

        def routes(cross, j):
            found = []
            for i in range(seq):
                core, chip = i % CORES, i // CORES
                kind = core ^ cross
                x, y = chip % side, chip // side
                if kind == 0:
                    x ^= j
                else:
                    y ^= j
                found.append((i, (y * side + x) * CORES + kind))
            return found

        sets = column_sets(side)
        moved_grad, moved_attn = [column[0]], [attn]
        for i in range(1, len(sets)):
            moved_attn.append(lax.ppermute(attn, "seq", routes(*sets[i])))
            moved_grad.append(lax.ppermute(column[i], "seq", routes(*sets[i])))
        partial = weight_grad(moved_attn, moved_grad, side, width)

        def final_routes(t):
            found = []
            for i in range(seq):
                core, chip = i % CORES, i // CORES
                x, y = chip % side, chip // side
                if core == 0:
                    y ^= t
                else:
                    x ^= t
                found.append((i, (y * side + x) * CORES + core))
            return found

        grad_wo = partial[0]
        for t in range(1, side):
            moved = lax.ppermute(partial[t], "seq", final_routes(t))
            grad_wo = grad_wo + moved
    else:
        grad_full = lax.all_gather(grad_out, "head", axis=1, tiled=True)
        grad_wo = lax.psum_scatter(
            jnp.dot(grad_full.T, attn.T, precision=lax.Precision.HIGHEST),
            "seq",
            scatter_dimension=0,
            tiled=True,
        ).T

    *carried, send = backward_far(queries, d_attn, weights, inv, pieces, score_scale)
    swapped = swap(send)
    grad_q, keep = backward_near(queries, d_attn, weights, inv, carried, pieces[:-1], score_scale)
    summed = (keep + swapped).reshape(chips, tokens, 2 * HD)
    grad_kv = summed[0]
    for j in range(1, chips):
        moved = to_chip(summed[j], j)
        grad_kv = grad_kv + moved
    return (grad_q, grad_kv[:, :HD], grad_kv[:, HD:], grad_wo)


def solution(mesh):
    in_specs = (
        P("seq", "head"),
        P("seq", "head"),
        P("seq", "head"),
        P("seq", "head"),
        P("head", None),
    )
    out_specs = (P("seq", "head"), P("seq", "head"), P("seq", "head"), P("head", "seq"))
    return jax.shard_map(
        body,
        mesh=mesh,
        in_specs=in_specs,
        out_specs=out_specs,
        check_vma=False,
    )
```

```python
import functools
import math

import jax
import jax.numpy as jnp
from jax import lax
from jax.experimental import pallas as pl
from jax.experimental.pallas import tpu as pltpu
from jax.sharding import PartitionSpec as P

HD = 128
GROUP = 4
CORES = 2
MASKED = -1e30
F32 = jnp.float32
BF16 = jnp.bfloat16

NN = (((1,), (0,)), ((), ()))
NT = (((1,), (1,)), ((), ()))


def mm(a, b, dims=NN):
    return lax.dot_general(a, b, dims, preferred_element_type=F32)


def two(x):
    hi = x.astype(BF16)
    return hi, (x - hi.astype(F32)).astype(BF16)


def three(x):
    first = x.astype(BF16)
    rest = x - first.astype(F32)
    second = rest.astype(BF16)
    return first, second, (rest - second.astype(F32)).astype(BF16)


def cost(flops, size):
    return pl.CostEstimate(flops=flops, transcendentals=0, bytes_accessed=size)


def params(held=0):
    return pltpu.CompilerParams(vmem_limit_bytes=(12 << 20) + held)


def load_blocks(refs, dst, column):
    row = 0
    for ref in refs:
        count = ref.shape[0]
        dst[row : row + count, :] = ref[:, column : column + HD]
        row += count


def pack_kernel(keys_ref, values_ref, out_ref, sem):
    copies = [
        pltpu.make_async_copy(ref, out_ref.at[:, i * HD : (i + 1) * HD], sem.at[i])
        for i, ref in enumerate((keys_ref, values_ref))
    ]
    for copy in copies:
        copy.start()
    for copy in copies:
        copy.wait()


def pack(keys, values):
    return pl.pallas_call(
        pack_kernel,
        out_shape=jax.ShapeDtypeStruct((keys.shape[0], 2 * HD), F32),
        in_specs=[pl.BlockSpec(memory_space=pl.ANY)] * 2,
        scratch_shapes=[pltpu.SemaphoreType.DMA((2,))],
        name="pack",
    )(keys, values)


def forward_kernel(score_scale, q_ref, *refs):
    pieces = refs[:-6]
    attn_ref, exp_ref, inv_ref, keys, values, score = refs[-6:]
    tokens = q_ref.shape[0]
    rows = GROUP * tokens
    total = keys.shape[0]
    blocks = total // tokens
    chips = blocks // CORES
    me = lax.axis_index("seq")
    load_blocks(pieces, keys, 0)
    load_blocks(pieces, values, HD)
    q1, q2, q3 = three(stacked_queries(q_ref))
    q11 = jnp.concatenate([q1, q1], axis=1)
    q22 = jnp.concatenate([q2, q2], axis=1)
    q13 = jnp.concatenate([q1, q3], axis=1)
    key_row = lax.broadcasted_iota(jnp.int32, (tokens, rows), 0)
    query_row = lax.broadcasted_iota(jnp.int32, (tokens, rows), 1) % tokens
    offset = key_row - query_row

    def scores(b, top):
        own = (b // chips) ^ (me % CORES)
        block = ((me // CORES) ^ (b % chips)) * CORES + own
        at = pl.ds(pl.multiple_of(b * tokens, tokens), tokens)
        k1, k2, k3 = three(keys[at, :])
        k12 = jnp.concatenate([k1, k2], axis=1)
        k31 = jnp.concatenate([k3, k1], axis=1)
        s = mm(k31, q13, NT) + mm(k12, q22, NT) + mm(k12, q11, NT)
        s = jnp.where(offset <= (me - block) * tokens, s * score_scale, MASKED)
        score[at, :] = s
        return jnp.maximum(top, jnp.max(s, axis=0, keepdims=True))

    top = lax.fori_loop(0, blocks, scores, jnp.full((1, rows), MASKED, F32), unroll=2)

    def weigh(b, state):
        norm, acc = state
        at = pl.ds(pl.multiple_of(b * tokens, tokens), tokens)
        e = jnp.exp(score[at, :] - top)
        exp_ref[at, :] = e
        eh, el = two(e)
        vh, vl = two(values[at, :].T)
        both = mm(jnp.concatenate([vh, vl], axis=0), eh)
        acc = acc + (both[:HD] + both[HD:] + mm(vh, el))
        return norm + jnp.sum(e, axis=0, keepdims=True), acc

    norm, acc = lax.fori_loop(
        0, blocks, weigh, (jnp.zeros((1, rows), F32), jnp.zeros((HD, rows), F32)), unroll=2
    )
    inv = 1.0 / norm
    inv_ref[...] = jnp.broadcast_to(inv, inv_ref.shape)
    out = acc * inv
    for g in range(GROUP):
        attn_ref[g * HD : (g + 1) * HD, :] = out[:, g * tokens : (g + 1) * tokens]


def forward(q, pieces, total, score_scale):
    tokens = q.shape[0]
    rows = GROUP * tokens
    return pl.pallas_call(
        functools.partial(forward_kernel, score_scale),
        out_shape=(
            jax.ShapeDtypeStruct((GROUP * HD, tokens), F32),
            jax.ShapeDtypeStruct((total, rows), F32),
            jax.ShapeDtypeStruct((8, rows), F32),
        ),
        scratch_shapes=[
            pltpu.VMEM((total, HD), F32),
            pltpu.VMEM((total, HD), F32),
            pltpu.VMEM((total, rows), F32),
        ],
        compiler_params=params(12 * total * rows),
        cost_estimate=cost(36 * total * rows * HD, 8 * total * rows),
        name="attn_fwd",
    )(q, *pieces)


def stacked_queries(q_ref):
    return jnp.concatenate([q_ref[:, g * HD : (g + 1) * HD] for g in range(GROUP)], axis=0)


def stacked_grads(d_ref):
    return jnp.concatenate([d_ref[g * HD : (g + 1) * HD, :] for g in range(GROUP)], axis=1)


def key_grads(score_scale, first, q, d, exp_ref, inv, dp_ref, delta, keys, out_ref, acc):
    rows = q.shape[0]
    tokens = rows // GROUP
    qh, ql = two(q)
    qhl = jnp.concatenate([qh, ql], axis=1)
    dh, dl = two(d)
    dhl = jnp.concatenate([dh, dl], axis=0)

    def grads(b, acc):
        to = pl.ds(pl.multiple_of(b * tokens, tokens), tokens)
        at = pl.ds(pl.multiple_of(first + b * tokens, tokens), tokens)
        p = exp_ref[at, :] * inv
        ds = p * (dp_ref[at, :] - delta) * score_scale
        ph, plo = two(p)
        sh, sl = two(ds)
        kh, kl = two(keys[to, :].T)
        both = mm(jnp.concatenate([kh, kl], axis=0), sh)
        acc = acc + (both[:HD] + both[HD:] + mm(kh, sl))
        dk = mm(sh, qhl)
        out_ref[to, 0:HD] = dk[:, :HD] + dk[:, HD:] + mm(sl, qh)
        dv = mm(ph, dhl, NT)
        out_ref[to, HD : 2 * HD] = dv[:, :HD] + dv[:, HD:] + mm(plo, dh, NT)
        return acc

    return lax.fori_loop(0, out_ref.shape[0] // tokens, grads, acc, unroll=2)


def backward_far_kernel(score_scale, q_ref, d_ref, exp_ref, inv_ref, *refs):
    pieces = refs[:-6]
    acc_ref, dp_ref, delta_ref, send_ref, keys, values = refs[-6:]
    tokens = q_ref.shape[0]
    rows = GROUP * tokens
    total = values.shape[0]
    load_blocks(pieces[-1:], keys, 0)
    load_blocks(pieces, values, HD)
    d = stacked_grads(d_ref)
    dh, dl = two(d)
    dhh = jnp.concatenate([dh, dh], axis=0)
    inv = inv_ref[0:1, :]

    def probs(b, delta):
        at = pl.ds(pl.multiple_of(b * tokens, tokens), tokens)
        vh, vl = two(values[at, :])
        dp = mm(vh, dl) + mm(jnp.concatenate([vh, vl], axis=1), dhh)
        dp_ref[at, :] = dp
        return delta + jnp.sum(exp_ref[at, :] * dp, axis=0, keepdims=True)

    delta = lax.fori_loop(0, total // tokens, probs, jnp.zeros((1, rows), F32), unroll=2) * inv
    delta_ref[...] = jnp.broadcast_to(delta, delta_ref.shape)
    acc_ref[...] = key_grads(
        score_scale,
        total - send_ref.shape[0],
        stacked_queries(q_ref),
        d,
        exp_ref,
        inv,
        dp_ref,
        delta,
        keys,
        send_ref,
        jnp.zeros((HD, rows), F32),
    )


def backward_near_kernel(
    score_scale, q_ref, d_ref, exp_ref, inv_ref, acc_ref, dp_ref, delta_ref, *refs
):
    pieces = refs[:-3]
    dq_ref, keep_ref, keys = refs[-3:]
    tokens = q_ref.shape[0]
    load_blocks(pieces, keys, 0)
    acc = key_grads(
        score_scale,
        0,
        stacked_queries(q_ref),
        stacked_grads(d_ref),
        exp_ref,
        inv_ref[0:1, :],
        dp_ref,
        delta_ref[0:1, :],
        keys,
        keep_ref,
        acc_ref[...],
    )
    for g in range(GROUP):
        dq_ref[:, g * HD : (g + 1) * HD] = acc[:, g * tokens : (g + 1) * tokens].T


def backward_far(q, d_attn, weights, inv, pieces, score_scale):
    total, rows = weights.shape
    half = total // CORES
    return pl.pallas_call(
        functools.partial(backward_far_kernel, score_scale),
        out_shape=(
            jax.ShapeDtypeStruct((HD, rows), F32),
            jax.ShapeDtypeStruct((total, rows), F32),
            jax.ShapeDtypeStruct((8, rows), F32),
            jax.ShapeDtypeStruct((half, 2 * HD), F32),
        ),
        scratch_shapes=[pltpu.VMEM((half, HD), F32), pltpu.VMEM((total, HD), F32)],
        compiler_params=params(12 * total * rows),
        cost_estimate=cost(24 * total * rows * HD, 8 * total * rows),
        name="attn_bwd_far",
    )(q, d_attn, weights, inv, *pieces)


def backward_near(q, d_attn, weights, inv, carried, pieces, score_scale):
    total, rows = weights.shape
    half = total // CORES
    return pl.pallas_call(
        functools.partial(backward_near_kernel, score_scale),
        out_shape=(
            jax.ShapeDtypeStruct(q.shape, F32),
            jax.ShapeDtypeStruct((half, 2 * HD), F32),
        ),
        scratch_shapes=[pltpu.VMEM((half, HD), F32)],
        compiler_params=params(12 * total * rows),
        cost_estimate=cost(18 * total * rows * HD, 8 * total * rows),
        name="attn_bwd_near",
    )(q, d_attn, weights, inv, *carried, *pieces)


def project_kernel(new, old, side, width, *refs):
    refs = list(refs)

    def take(count):
        taken = refs[:count]
        del refs[:count]
        return taken

    (w_ref,) = take(1)
    fresh = [take(count) for _, count in new]
    stale = [take(count) for _, count in old] if side else []
    carried = take(1) if old else []
    (d_ref,) = take(1)
    outs = take(len(column_sets(side))) if side else []
    weights, sem = take(2)
    rows, tokens = d_ref.shape
    part = weights.shape[2]
    me = lax.axis_index("head")

    def block(copies):
        return functools.reduce(jnp.add, [ref[...] for ref in copies])

    def column(offset):
        return pl.ds(pl.multiple_of((me ^ offset) * part, part), part)

    copies = [
        pltpu.make_async_copy(w_ref.at[:, column(offset)], weights.at[i], sem.at[i])
        for i, (offset, _) in enumerate(new)
    ]
    for copy in copies:
        copy.start()
    if side:
        (full,) = take(1)
        for piece, offset in zip(stale + fresh, [o for o, _ in old + new]):
            full[:, column(offset)] = block(piece)
        seq = lax.axis_index("seq")
        core = seq % CORES
        chip = seq // CORES
        x, y = chip % side, chip // side
        for out, (other_core, j) in zip(outs, column_sets(side)):
            kind = core ^ other_core
            fixed = jnp.where(kind == 0, x, y) ^ j
            moving = jnp.where(kind == 0, y, x)
            for t in range(side):
                i = moving ^ t
                index = jnp.where(kind == 0, i * side + fixed, fixed * side + i)
                at = pl.multiple_of((index * CORES + kind) * width, width)
                out[:, t * width : (t + 1) * width] = full[:, pl.ds(at, width)]
    step = rows // 2
    for i, piece in enumerate(fresh):
        g_hi, g_lo = two(block(piece))
        g_both = jnp.concatenate([g_hi, g_lo], axis=0)
        copies[i].wait()
        for row in range(0, rows, step):
            at = slice(row, row + step)
            w_hi, w_lo = two(weights[i, at, :])
            both = mm(w_hi, g_both, NT)
            value = both[:, :tokens] + both[:, tokens:] + mm(w_lo, g_hi, NT)
            if i or carried:
                value = value + (d_ref if i else carried[0])[at, :]
            d_ref[at, :] = value


def column_sets(side):
    sets = [(0, 0)]
    for j in range(side):
        if j:
            sets.append((0, j))
        sets.append((1, j))
    return sets


def project(out_weight, blocks, new, old, carried, side, width):
    heads = lax.axis_size("head")
    rows, columns = out_weight.shape
    tokens = blocks[0][0].shape[0]
    part = columns // heads
    offsets = len(new)
    shapes = [jax.ShapeDtypeStruct((rows, tokens), F32)]
    scratch = [
        pltpu.VMEM((offsets, rows, part), F32),
        pltpu.SemaphoreType.DMA((offsets,)),
    ]
    operands = [copy for d in new for copy in blocks[d]]
    if side:
        shapes += [jax.ShapeDtypeStruct((tokens, side * width), F32)] * len(column_sets(side))
        scratch.append(pltpu.VMEM((tokens, columns), F32))
        operands += [copy for d in old for copy in blocks[d]]
    if old:
        operands.append(carried)

    def counted(distances):
        return [(d, len(blocks[d])) for d in distances]

    return pl.pallas_call(
        functools.partial(project_kernel, counted(new), counted(old), side, width),
        out_shape=tuple(shapes),
        in_specs=[pl.BlockSpec(memory_space=pltpu.HBM)]
        + [pl.BlockSpec(memory_space=pltpu.VMEM)] * len(operands),
        scratch_shapes=scratch,
        compiler_params=params(),
        cost_estimate=cost(24 * tokens * rows * part * offsets, 4 * rows * part * offsets),
        name="project",
    )(out_weight, *operands)


def weight_kernel(count, *refs):
    attn = refs[:count]
    grad = refs[count : 2 * count]
    outs = refs[2 * count :]
    width = outs[0].shape[1]
    a_hi, a_lo = two(jnp.concatenate([ref[...] for ref in attn], axis=1))
    for t, out in enumerate(outs):
        cut = slice(t * width, (t + 1) * width)
        g_hi, g_lo = two(jnp.concatenate([ref[:, cut] for ref in grad], axis=0))
        out[...] = mm(a_hi, g_lo) + mm(a_lo, g_hi) + mm(a_hi, g_hi)


def weight_grad(attn, grad, side, width):
    rows = attn[0].shape[0]
    return pl.pallas_call(
        functools.partial(weight_kernel, len(attn)),
        out_shape=(jax.ShapeDtypeStruct((rows, width), F32),) * side,
        compiler_params=params(),
        cost_estimate=cost(2 * rows * rows * width * side, 8 * rows * width * side),
        name="weight_grad",
    )(*attn, *grad)


def body(queries, keys, values, grad_out, out_weight):
    tokens = queries.shape[0]
    seq = lax.axis_size("seq")
    heads = lax.axis_size("head")
    chips = seq // CORES
    total = seq * tokens
    width = out_weight.shape[1] // seq
    score_scale = 1.0 / math.sqrt(HD)
    side = math.isqrt(chips)
    exchange = side * side == chips and width % 128 == 0

    def swap(block):
        return lax.ppermute(block, "seq", [(i, i ^ 1) for i in range(seq)])

    def to_chip(block, j):
        return lax.ppermute(block, "seq", [(i, i ^ (CORES * j)) for i in range(seq)])

    def along(block, route):
        return lax.ppermute(block, "head", route)

    by_distance = {0: (grad_out,)}
    for d in range(1, heads):
        if d + 1 < heads or heads != GROUP:
            by_distance[d] = (along(grad_out, [(i, i ^ d) for i in range(heads)]),)
    if heads == GROUP:
        middle = along(grad_out, [(1, 2), (2, 1)])
        ends = along(by_distance[2][0], [(1, 0), (2, 3)])
        by_distance[3] = middle, ends

    own = pack(keys, values)
    same = [own]
    for j in range(1, chips):
        same.append(to_chip(own, j))
    pieces = same + [swap(jnp.concatenate(same, axis=0))]

    attn, weights, inv = forward(queries, pieces, total, score_scale)
    d_attn, column = None, ()
    seen = []
    for fresh in ([0], [1], list(range(2, heads))):
        final = fresh[-1] == heads - 1
        d_attn, *column = project(
            out_weight,
            by_distance,
            fresh,
            seen,
            d_attn,
            side if exchange and final else 0,
            width,
        )
        seen = seen + fresh
        if final:
            break

    if exchange:

        def routes(cross, j):
            found = []
            for i in range(seq):
                core, chip = i % CORES, i // CORES
                kind = core ^ cross
                x, y = chip % side, chip // side
                if kind == 0:
                    x ^= j
                else:
                    y ^= j
                found.append((i, (y * side + x) * CORES + kind))
            return found

        sets = column_sets(side)
        moved_grad, moved_attn = [column[0]], [attn]
        for i in range(1, len(sets)):
            moved_attn.append(lax.ppermute(attn, "seq", routes(*sets[i])))
            moved_grad.append(lax.ppermute(column[i], "seq", routes(*sets[i])))
        partial = weight_grad(moved_attn, moved_grad, side, width)

        def final_routes(t):
            found = []
            for i in range(seq):
                core, chip = i % CORES, i // CORES
                x, y = chip % side, chip // side
                if core == 0:
                    y ^= t
                else:
                    x ^= t
                found.append((i, (y * side + x) * CORES + core))
            return found

        grad_wo = partial[0]
        for t in range(1, side):
            moved = lax.ppermute(partial[t], "seq", final_routes(t))
            grad_wo = grad_wo + moved
    else:
        grad_full = lax.all_gather(grad_out, "head", axis=1, tiled=True)
        grad_wo = lax.psum_scatter(
            jnp.dot(grad_full.T, attn.T, precision=lax.Precision.HIGHEST),
            "seq",
            scatter_dimension=0,
            tiled=True,
        ).T

    *carried, send = backward_far(queries, d_attn, weights, inv, pieces, score_scale)
    swapped = swap(send)
    grad_q, keep = backward_near(queries, d_attn, weights, inv, carried, pieces[:-1], score_scale)
    summed = (keep + swapped).reshape(chips, tokens, 2 * HD)
    grad_kv = summed[0]
    for j in range(1, chips):
        moved = to_chip(summed[j], j)
        grad_kv = grad_kv + moved
    return (grad_q, grad_kv[:, :HD], grad_kv[:, HD:], grad_wo)


def solution(mesh):
    in_specs = (
        P("seq", "head"),
        P("seq", "head"),
        P("seq", "head"),
        P("seq", "head"),
        P("head", None),
    )
    out_specs = (P("seq", "head"), P("seq", "head"), P("seq", "head"), P("head", "seq"))
    return jax.shard_map(
        body,
        mesh=mesh,
        in_specs=in_specs,
        out_specs=out_specs,
        check_vma=False,
    )
```

```python
import functools
import math

import jax
import jax.numpy as jnp
from jax import lax
from jax.experimental import pallas as pl
from jax.experimental.pallas import tpu as pltpu
from jax.sharding import PartitionSpec as P

HD = 128
GROUP = 4
CORES = 2
MASKED = -1e30
F32 = jnp.float32
BF16 = jnp.bfloat16

NN = (((1,), (0,)), ((), ()))
NT = (((1,), (1,)), ((), ()))


def mm(a, b, dims=NN):
    return lax.dot_general(a, b, dims, preferred_element_type=F32)


def two(x):
    hi = x.astype(BF16)
    return hi, (x - hi.astype(F32)).astype(BF16)


def three(x):
    first = x.astype(BF16)
    rest = x - first.astype(F32)
    second = rest.astype(BF16)
    return first, second, (rest - second.astype(F32)).astype(BF16)


def cost(flops, size):
    return pl.CostEstimate(flops=flops, transcendentals=0, bytes_accessed=size)


def params(held=0):
    return pltpu.CompilerParams(vmem_limit_bytes=(12 << 20) + held)


def in_hbm(x):
    return pltpu.with_memory_space_constraint(x, pltpu.HBM)


def load_blocks(refs, dst, column):
    row = 0
    for ref in refs:
        count = ref.shape[0]
        dst[row : row + count, :] = ref[:, column : column + HD]
        row += count


def pack_kernel(keys_ref, values_ref, grad_ref, out_ref, upper_ref, lower_ref, sem):
    count = upper_ref.shape[0]
    pairs = (
        (keys_ref, out_ref.at[:, :HD]),
        (values_ref, out_ref.at[:, HD:]),
        (grad_ref.at[:count], upper_ref),
        (grad_ref.at[count:], lower_ref),
    )
    copies = [pltpu.make_async_copy(a, b, sem.at[i]) for i, (a, b) in enumerate(pairs)]
    for copy in copies:
        copy.start()
    for copy in copies:
        copy.wait()


def pack(keys, values, grad_out):
    tokens, columns = grad_out.shape
    part = jax.ShapeDtypeStruct((tokens // 2, columns), F32)
    return pl.pallas_call(
        pack_kernel,
        out_shape=(jax.ShapeDtypeStruct((tokens, 2 * HD), F32), part, part),
        in_specs=[pl.BlockSpec(memory_space=pltpu.HBM)] * 3,
        scratch_shapes=[pltpu.SemaphoreType.DMA((4,))],
        compiler_params=params(),
        name="pack",
    )(*(in_hbm(x) for x in (keys, values, grad_out)))


def forward_kernel(score_scale, other, q_ref, *refs):
    if other:
        *pieces, top_ref, norm_ref, acc_ref, attn_ref, exp_ref, inv_ref, keys, values, score = refs
    else:
        *pieces, top_ref, norm_ref, acc_ref, exp_ref, keys, values, score = refs
    tokens = q_ref.shape[0]
    rows = GROUP * tokens
    blocks = keys.shape[0] // tokens
    me = lax.axis_index("seq")
    load_blocks(pieces, keys, 0)
    load_blocks(pieces, values, HD)
    q1, q2, q3 = three(stacked_queries(q_ref))
    q11 = jnp.concatenate([q1, q1], axis=1)
    q22 = jnp.concatenate([q2, q2], axis=1)
    q13 = jnp.concatenate([q1, q3], axis=1)
    key_row = lax.broadcasted_iota(jnp.int32, (tokens, rows), 0)
    query_row = lax.broadcasted_iota(jnp.int32, (tokens, rows), 1) % tokens
    offset = key_row - query_row

    def scores(b, top):
        block = ((me // CORES) ^ b) * CORES + ((me % CORES) ^ other)
        at = pl.ds(pl.multiple_of(b * tokens, tokens), tokens)
        k1, k2, k3 = three(keys[at, :])
        k12 = jnp.concatenate([k1, k2], axis=1)
        k31 = jnp.concatenate([k3, k1], axis=1)
        s = mm(k31, q13, NT) + mm(k12, q22, NT) + mm(k12, q11, NT)
        s = jnp.where(offset <= (me - block) * tokens, s * score_scale, MASKED)
        score[at, :] = s
        return jnp.maximum(top, jnp.max(s, axis=0, keepdims=True))

    before = top_ref[0:1, :] if other else jnp.full((1, rows), MASKED, F32)
    top = lax.fori_loop(0, blocks, scores, before, unroll=2)

    def weigh(b, state):
        norm, acc = state
        at = pl.ds(pl.multiple_of(b * tokens, tokens), tokens)
        e = jnp.exp(score[at, :] - top)
        exp_ref[at, :] = e
        eh, el = two(e)
        vh, vl = two(values[at, :].T)
        both = mm(jnp.concatenate([vh, vl], axis=0), eh)
        acc = acc + (both[:HD] + both[HD:] + mm(vh, el))
        return norm + jnp.sum(e, axis=0, keepdims=True), acc

    if other:
        factor = jnp.exp(before - top)
        start = norm_ref[0:1, :] * factor, acc_ref[...] * factor
    else:
        start = jnp.zeros((1, rows), F32), jnp.zeros((HD, rows), F32)
    norm, acc = lax.fori_loop(0, blocks, weigh, start, unroll=2)
    if other:
        inv = 1.0 / norm
        inv_ref[0:8, :] = jnp.broadcast_to(inv * factor, (8, rows))
        inv_ref[8:16, :] = jnp.broadcast_to(inv, (8, rows))
        out = acc * inv
        for g in range(GROUP):
            attn_ref[g * HD : (g + 1) * HD, :] = out[:, g * tokens : (g + 1) * tokens]
    else:
        top_ref[...] = jnp.broadcast_to(top, top_ref.shape)
        norm_ref[...] = jnp.broadcast_to(norm, norm_ref.shape)
        acc_ref[...] = acc


def forward(q, pieces, carried, score_scale):
    tokens = q.shape[0]
    rows = GROUP * tokens
    half = sum(piece.shape[0] for piece in pieces)
    weights = jax.ShapeDtypeStruct((half, rows), F32)
    row = jax.ShapeDtypeStruct((8, rows), F32)
    if carried:
        shapes = (
            jax.ShapeDtypeStruct((GROUP * HD, tokens), F32),
            weights,
            jax.ShapeDtypeStruct((16, rows), F32),
        )
    else:
        shapes = row, row, jax.ShapeDtypeStruct((HD, rows), F32), weights
    return pl.pallas_call(
        functools.partial(forward_kernel, score_scale, 1 if carried else 0),
        out_shape=shapes,
        scratch_shapes=[
            pltpu.VMEM((half, HD), F32),
            pltpu.VMEM((half, HD), F32),
            pltpu.VMEM((half, rows), F32),
        ],
        compiler_params=params(12 * half * rows),
        cost_estimate=cost(36 * half * rows * HD, 8 * half * rows),
        name="attn_fwd",
    )(q, *pieces, *carried)


def stacked_queries(q_ref):
    return jnp.concatenate([q_ref[:, g * HD : (g + 1) * HD] for g in range(GROUP)], axis=0)


def stacked_grads(d_ref):
    return jnp.concatenate([d_ref[g * HD : (g + 1) * HD, :] for g in range(GROUP)], axis=1)


def key_grads(score_scale, q, d, exp_ref, inv, dp_ref, delta, keys, out_ref, acc):
    rows = q.shape[0]
    tokens = rows // GROUP
    qh, ql = two(q)
    qhl = jnp.concatenate([qh, ql], axis=1)
    dh, dl = two(d)
    dhl = jnp.concatenate([dh, dl], axis=0)

    def grads(b, acc):
        at = pl.ds(pl.multiple_of(b * tokens, tokens), tokens)
        p = exp_ref[at, :] * inv
        ds = p * (dp_ref[at, :] - delta) * score_scale
        ph, plo = two(p)
        sh, sl = two(ds)
        kh, kl = two(keys[at, :].T)
        both = mm(jnp.concatenate([kh, kl], axis=0), sh)
        acc = acc + (both[:HD] + both[HD:] + mm(kh, sl))
        dk = mm(sh, qhl)
        out_ref[at, 0:HD] = dk[:, :HD] + dk[:, HD:] + mm(sl, qh)
        dv = mm(ph, dhl, NT)
        out_ref[at, HD : 2 * HD] = dv[:, :HD] + dv[:, HD:] + mm(plo, dh, NT)
        return acc

    return lax.fori_loop(0, out_ref.shape[0] // tokens, grads, acc, unroll=2)


def backward_far_kernel(score_scale, q_ref, d_ref, near_ref, far_ref, inv_ref, *refs):
    *pieces, acc_ref, dp_ref, delta_ref, send_ref, keys, values, far_dp = refs
    tokens = q_ref.shape[0]
    rows = GROUP * tokens
    half = keys.shape[0]
    load_blocks(pieces[-1:], keys, 0)
    load_blocks(pieces, values, HD)
    d = stacked_grads(d_ref)
    dh, dl = two(d)
    dhh = jnp.concatenate([dh, dh], axis=0)

    def probs(exp_ref, out_ref, first):
        def one(b, total):
            at = pl.ds(pl.multiple_of(b * tokens, tokens), tokens)
            vh, vl = two(values[pl.ds(pl.multiple_of(first + b * tokens, tokens), tokens), :])
            dp = mm(vh, dl) + mm(jnp.concatenate([vh, vl], axis=1), dhh)
            out_ref[at, :] = dp
            return total + jnp.sum(exp_ref[at, :] * dp, axis=0, keepdims=True)

        return lax.fori_loop(0, half // tokens, one, jnp.zeros((1, rows), F32), unroll=2)

    inv = inv_ref[8:9, :]
    delta = probs(near_ref, dp_ref, 0) * inv_ref[0:1, :] + probs(far_ref, far_dp, half) * inv
    delta_ref[...] = jnp.broadcast_to(delta, delta_ref.shape)
    acc_ref[...] = key_grads(
        score_scale,
        stacked_queries(q_ref),
        d,
        far_ref,
        inv,
        far_dp,
        delta,
        keys,
        send_ref,
        jnp.zeros((HD, rows), F32),
    )


def backward_near_kernel(
    score_scale, q_ref, d_ref, near_ref, inv_ref, acc_ref, dp_ref, delta_ref, *refs
):
    *pieces, dq_ref, keep_ref, keys = refs
    tokens = q_ref.shape[0]
    load_blocks(pieces, keys, 0)
    acc = key_grads(
        score_scale,
        stacked_queries(q_ref),
        stacked_grads(d_ref),
        near_ref,
        inv_ref[0:1, :],
        dp_ref,
        delta_ref[0:1, :],
        keys,
        keep_ref,
        acc_ref[...],
    )
    for g in range(GROUP):
        dq_ref[:, g * HD : (g + 1) * HD] = acc[:, g * tokens : (g + 1) * tokens].T


def backward_far(q, d_attn, near, far, inv, pieces, score_scale):
    half, rows = far.shape
    return pl.pallas_call(
        functools.partial(backward_far_kernel, score_scale),
        out_shape=(
            jax.ShapeDtypeStruct((HD, rows), F32),
            jax.ShapeDtypeStruct((half, rows), F32),
            jax.ShapeDtypeStruct((8, rows), F32),
            jax.ShapeDtypeStruct((half, 2 * HD), F32),
        ),
        scratch_shapes=[
            pltpu.VMEM((half, HD), F32),
            pltpu.VMEM((2 * half, HD), F32),
            pltpu.VMEM((half, rows), F32),
        ],
        compiler_params=params(24 * half * rows),
        cost_estimate=cost(48 * half * rows * HD, 16 * half * rows),
        name="attn_bwd_far",
    )(q, d_attn, near, far, inv, *pieces)


def backward_near(q, d_attn, near, inv, carried, pieces, score_scale):
    half, rows = near.shape
    return pl.pallas_call(
        functools.partial(backward_near_kernel, score_scale),
        out_shape=(
            jax.ShapeDtypeStruct(q.shape, F32),
            jax.ShapeDtypeStruct((half, 2 * HD), F32),
        ),
        scratch_shapes=[pltpu.VMEM((half, HD), F32)],
        compiler_params=params(12 * half * rows),
        cost_estimate=cost(36 * half * rows * HD, 8 * half * rows),
        name="attn_bwd_near",
    )(q, d_attn, near, inv, *carried, *pieces)


def project_kernel(new, old, side, width, *refs):
    refs = list(refs)

    def take(count):
        taken = refs[:count]
        del refs[:count]
        return taken

    (w_ref,) = take(1)
    fresh = [[take(n) for n in counts] for _, counts in new]
    stale = [[take(n) for n in counts] for _, counts in old] if side else []
    carried = take(1) if old else []
    (d_ref,) = take(1)
    outs = take(len(column_sets(side))) if side else []
    weights, sem = (w_ref, None) if old else take(2)
    heads, rows, part = weights.shape
    tokens = d_ref.shape[1]
    me = lax.axis_index("head")

    def block(copies):
        whole = [
            jnp.concatenate([ref[...] for ref in rows], axis=0) if len(rows) > 1 else rows[0][...]
            for rows in copies
        ]
        return functools.reduce(jnp.add, whole)

    def column(offset):
        return pl.ds(pl.multiple_of((me ^ offset) * part, part), part)

    copies = {}
    if not old:
        for d in range(heads):
            copies[d] = pltpu.make_async_copy(w_ref.at[:, column(d)], weights.at[d], sem.at[d])
            copies[d].start()
    if side:
        (full,) = take(1)
        for piece, offset in zip(stale + fresh, [o for o, _ in old + new]):
            full[:, column(offset)] = block(piece)
        seq = lax.axis_index("seq")
        core = seq % CORES
        chip = seq // CORES
        x, y = chip % side, chip // side
        for out, (other_core, j) in zip(outs, column_sets(side)):
            kind = core ^ other_core
            fixed = jnp.where(kind == 0, x, y) ^ j
            moving = jnp.where(kind == 0, y, x)
            for t in range(side):
                i = moving ^ t
                index = jnp.where(kind == 0, i * side + fixed, fixed * side + i)
                at = pl.multiple_of((index * CORES + kind) * width, width)
                out[:, t * width : (t + 1) * width] = full[:, pl.ds(at, width)]
    step = rows // 2
    for i, (piece, (d, _)) in enumerate(zip(fresh, new)):
        g_hi, g_lo = two(block(piece))
        g_both = jnp.concatenate([g_hi, g_lo], axis=0)
        if d in copies:
            copies.pop(d).wait()
        for row in range(0, rows, step):
            at = slice(row, row + step)
            w_hi, w_lo = two(weights[d, at, :])
            both = mm(w_hi, g_both, NT)
            value = both[:, :tokens] + both[:, tokens:] + mm(w_lo, g_hi, NT)
            if i or carried:
                value = value + (d_ref if i else carried[0])[at, :]
            d_ref[at, :] = value
    for copy in copies.values():
        copy.wait()


def column_sets(side):
    sets = [(0, 0)]
    for j in range(side):
        if j:
            sets.append((0, j))
        sets.append((1, j))
    return sets


def project(weight, blocks, new, old, carried, side, width):
    heads = lax.axis_size("head")
    tokens = sum(piece.shape[0] for piece in blocks[0][0])
    if old:
        _, rows, part = weight.shape
    else:
        rows, part = weight.shape[0], weight.shape[1] // heads
    shapes = [jax.ShapeDtypeStruct((rows, tokens), F32)]
    scratch = []
    operands = [piece for d in new for copy in blocks[d] for piece in copy]
    if side:
        shapes += [jax.ShapeDtypeStruct((tokens, side * width), F32)] * len(column_sets(side))
        scratch.append(pltpu.VMEM((tokens, heads * part), F32))
        operands += [piece for d in old for copy in blocks[d] for piece in copy]
    if old:
        operands.append(carried)
    else:
        weight = in_hbm(weight)
        shapes.append(jax.ShapeDtypeStruct((heads, rows, part), F32))
        scratch.append(pltpu.SemaphoreType.DMA((heads,)))

    def counted(distances):
        return [(d, tuple(len(copy) for copy in blocks[d])) for d in distances]

    return pl.pallas_call(
        functools.partial(project_kernel, counted(new), counted(old), side, width),
        out_shape=tuple(shapes),
        in_specs=[pl.BlockSpec(memory_space=pltpu.VMEM if old else pltpu.HBM)]
        + [pl.BlockSpec(memory_space=pltpu.VMEM)] * len(operands),
        scratch_shapes=scratch,
        compiler_params=params(8 * heads * rows * part),
        cost_estimate=cost(24 * tokens * rows * part * len(new), 4 * rows * part * len(new)),
        name="project",
    )(weight, *operands)


def weight_kernel(count, *refs):
    attn = refs[:count]
    grad = refs[count : 2 * count]
    outs = refs[2 * count :]
    width = outs[0].shape[1]
    a_hi, a_lo = two(jnp.concatenate([ref[...] for ref in attn], axis=1))
    for t, out in enumerate(outs):
        cut = slice(t * width, (t + 1) * width)
        g_hi, g_lo = two(jnp.concatenate([ref[:, cut] for ref in grad], axis=0))
        out[...] = mm(a_hi, g_lo) + mm(a_lo, g_hi) + mm(a_hi, g_hi)


def weight_grad(attn, grad, side, width):
    rows = attn[0].shape[0]
    return pl.pallas_call(
        functools.partial(weight_kernel, len(attn)),
        out_shape=(jax.ShapeDtypeStruct((rows, width), F32),) * side,
        compiler_params=params(),
        cost_estimate=cost(2 * rows * rows * width * side, 8 * rows * width * side),
        name="weight_grad",
    )(*attn, *grad)


def body(queries, keys, values, grad_out, out_weight):
    tokens = queries.shape[0]
    seq = lax.axis_size("seq")
    heads = lax.axis_size("head")
    chips = seq // CORES
    width = out_weight.shape[1] // seq
    score_scale = 1.0 / math.sqrt(HD)
    side = math.isqrt(chips)
    exchange = side * side == chips and width % 128 == 0

    def swap(block):
        return lax.ppermute(block, "seq", [(i, i ^ 1) for i in range(seq)])

    def to_chip(block, j):
        return lax.ppermute(block, "seq", [(i, i ^ (CORES * j)) for i in range(seq)])

    def along(block, route):
        return lax.ppermute(block, "head", route)

    own, upper, lower = pack(keys, values, grad_out)
    by_distance = {0: ((upper, lower),)}
    for d in range(1, heads):
        pairs = [(i, i ^ d) for i in range(heads)]
        if heads != GROUP or d == 1:
            by_distance[d] = ((along(grad_out, pairs),),)
        elif d == 2:
            by_distance[d] = ((along(upper, pairs), along(lower, pairs)),)
        else:
            ends = [(1, 0), (2, 3)]
            ((near_upper, near_lower),) = by_distance[2]
            by_distance[d] = (
                (along(grad_out, [(1, 2), (2, 1)]),),
                (along(near_upper, ends), along(near_lower, ends)),
            )

    same = [own]
    for j in range(1, chips):
        same.append(to_chip(own, j))
    pieces = same + [swap(jnp.concatenate(same, axis=0))]

    *carried, near = forward(queries, same, (), score_scale)
    attn, far, inv = forward(queries, pieces[-1:], carried, score_scale)
    weight, d_attn, column = out_weight, None, ()
    seen = []
    for fresh in ([0], [1], list(range(2, heads))):
        final = fresh[-1] == heads - 1
        d_attn, *column = project(
            weight, by_distance, fresh, seen, d_attn, side if exchange and final else 0, width
        )
        if not seen:
            weight = column.pop()
        seen = seen + fresh
        if final:
            break

    if exchange:

        def routes(cross, j):
            found = []
            for i in range(seq):
                core, chip = i % CORES, i // CORES
                kind = core ^ cross
                x, y = chip % side, chip // side
                if kind == 0:
                    x ^= j
                else:
                    y ^= j
                found.append((i, (y * side + x) * CORES + kind))
            return found

        sets = column_sets(side)
        moved_grad, moved_attn = [column[0]], [attn]
        for i in range(1, len(sets)):
            moved_attn.append(lax.ppermute(attn, "seq", routes(*sets[i])))
            moved_grad.append(lax.ppermute(column[i], "seq", routes(*sets[i])))
        partial = weight_grad(moved_attn, moved_grad, side, width)

        def final_routes(t):
            found = []
            for i in range(seq):
                core, chip = i % CORES, i // CORES
                x, y = chip % side, chip // side
                if core == 0:
                    y ^= t
                else:
                    x ^= t
                found.append((i, (y * side + x) * CORES + core))
            return found

        grad_wo = partial[0]
        for t in range(1, side):
            moved = lax.ppermute(partial[t], "seq", final_routes(t))
            grad_wo = grad_wo + moved
    else:
        grad_full = lax.all_gather(grad_out, "head", axis=1, tiled=True)
        grad_wo = lax.psum_scatter(
            jnp.dot(grad_full.T, attn.T, precision=lax.Precision.HIGHEST),
            "seq",
            scatter_dimension=0,
            tiled=True,
        ).T

    *carried, send = backward_far(queries, d_attn, near, far, inv, pieces, score_scale)
    swapped = swap(send)
    grad_q, keep = backward_near(queries, d_attn, near, inv, carried, same, score_scale)
    summed = (keep + swapped).reshape(chips, tokens, 2 * HD)
    grad_kv = summed[0]
    for j in range(1, chips):
        moved = to_chip(summed[j], j)
        grad_kv = grad_kv + moved
    return (grad_q, grad_kv[:, :HD], grad_kv[:, HD:], grad_wo)


def solution(mesh):
    in_specs = (
        P("seq", "head"),
        P("seq", "head"),
        P("seq", "head"),
        P("seq", "head"),
        P("head", None),
    )
    out_specs = (P("seq", "head"), P("seq", "head"), P("seq", "head"), P("head", "seq"))
    return jax.shard_map(
        body,
        mesh=mesh,
        in_specs=in_specs,
        out_specs=out_specs,
        check_vma=False,
    )
```

```python
import functools
import math

import jax
import jax.numpy as jnp
from jax import lax
from jax.experimental import pallas as pl
from jax.experimental.pallas import tpu as pltpu
from jax.sharding import PartitionSpec as P

HD = 128
GROUP = 4
CORES = 2
MASKED = -1e30
STEP = 4
F32 = jnp.float32
BF16 = jnp.bfloat16

NN = (((1,), (0,)), ((), ()))
NT = (((1,), (1,)), ((), ()))


def mm(a, b, dims=NN):
    return lax.dot_general(a, b, dims, preferred_element_type=F32)


def two(x):
    hi = x.astype(BF16)
    return hi, (x - hi.astype(F32)).astype(BF16)


def three(x):
    first = x.astype(BF16)
    rest = x - first.astype(F32)
    second = rest.astype(BF16)
    return first, second, (rest - second.astype(F32)).astype(BF16)


def cost(flops, size):
    return pl.CostEstimate(flops=flops, transcendentals=0, bytes_accessed=size)


def params(held=0):
    return pltpu.CompilerParams(vmem_limit_bytes=(12 << 20) + held)


def in_hbm(x):
    return pltpu.with_memory_space_constraint(x, pltpu.HBM)


def key_step(count, tokens):
    return next(tokens * n for n in (STEP, 2, 1) if count % (tokens * n) == 0)


def load_blocks(refs, dst, column):
    row = 0
    for ref in refs:
        count = ref.shape[0]
        dst[row : row + count, :] = ref[:, column : column + HD]
        row += count


def pack_kernel(keys_ref, values_ref, grad_ref, out_ref, upper_ref, lower_ref, sem):
    count = upper_ref.shape[0]
    pairs = (
        (keys_ref, out_ref.at[:, :HD]),
        (values_ref, out_ref.at[:, HD:]),
        (grad_ref.at[:count], upper_ref),
        (grad_ref.at[count:], lower_ref),
    )
    copies = [pltpu.make_async_copy(a, b, sem.at[i]) for i, (a, b) in enumerate(pairs)]
    for copy in copies:
        copy.start()
    for copy in copies:
        copy.wait()


def pack(keys, values, grad_out):
    tokens, columns = grad_out.shape
    part = jax.ShapeDtypeStruct((tokens // 2, columns), F32)
    return pl.pallas_call(
        pack_kernel,
        out_shape=(jax.ShapeDtypeStruct((tokens, 2 * HD), F32), part, part),
        in_specs=[pl.BlockSpec(memory_space=pltpu.HBM)] * 3,
        scratch_shapes=[pltpu.SemaphoreType.DMA((4,))],
        compiler_params=params(),
        name="pack",
    )(*(in_hbm(x) for x in (keys, values, grad_out)))


def forward_kernel(score_scale, other, q_ref, *refs):
    if other:
        *pieces, top_ref, norm_ref, acc_ref, attn_ref, exp_ref, inv_ref, keys, values, score = refs
    else:
        *pieces, top_ref, norm_ref, acc_ref, exp_ref, keys, values, score = refs
    tokens = q_ref.shape[0]
    rows = GROUP * tokens
    step = key_step(keys.shape[0], tokens)
    steps = keys.shape[0] // step
    me = lax.axis_index("seq")
    load_blocks(pieces, keys, 0)
    load_blocks(pieces, values, HD)
    q1, q2, q3 = three(stacked_queries(q_ref))
    q11 = jnp.concatenate([q1, q1], axis=1)
    q22 = jnp.concatenate([q2, q2], axis=1)
    q13 = jnp.concatenate([q1, q3], axis=1)
    key_row = lax.broadcasted_iota(jnp.int32, (tokens, rows), 0)
    query_row = lax.broadcasted_iota(jnp.int32, (tokens, rows), 1) % tokens
    offset = key_row - query_row

    def scores(b, top):
        k1, k2, k3 = three(keys[pl.ds(pl.multiple_of(b * step, step), step), :])
        k12 = jnp.concatenate([k1, k2], axis=1)
        k31 = jnp.concatenate([k3, k1], axis=1)
        found = mm(k31, q13, NT) + mm(k12, q22, NT) + mm(k12, q11, NT)
        for i in range(step // tokens):
            which = b * (step // tokens) + i
            block = ((me // CORES) ^ which) * CORES + ((me % CORES) ^ other)
            s = found[i * tokens : (i + 1) * tokens] * score_scale
            s = jnp.where(offset <= (me - block) * tokens, s, MASKED)
            score[pl.ds(pl.multiple_of(which * tokens, tokens), tokens), :] = s
            top = jnp.maximum(top, jnp.max(s, axis=0, keepdims=True))
        return top

    before = top_ref[0:1, :] if other else jnp.full((1, rows), MASKED, F32)
    top = lax.fori_loop(0, steps, scores, before)

    def weigh(b, state):
        norm, acc = state
        at = pl.ds(pl.multiple_of(b * step, step), step)
        e = jnp.exp(score[at, :] - top)
        exp_ref[at, :] = e
        eh, el = two(e)
        vh, vl = two(values[at, :].T)
        both = mm(jnp.concatenate([vh, vl], axis=0), eh)
        acc = acc + (both[:HD] + both[HD:] + mm(vh, el))
        return norm + jnp.sum(e, axis=0, keepdims=True), acc

    if other:
        factor = jnp.exp(before - top)
        start = norm_ref[0:1, :] * factor, acc_ref[...] * factor
    else:
        start = jnp.zeros((1, rows), F32), jnp.zeros((HD, rows), F32)
    norm, acc = lax.fori_loop(0, steps, weigh, start)
    if other:
        inv = 1.0 / norm
        inv_ref[0:8, :] = jnp.broadcast_to(inv * factor, (8, rows))
        inv_ref[8:16, :] = jnp.broadcast_to(inv, (8, rows))
        out = acc * inv
        for g in range(GROUP):
            attn_ref[g * HD : (g + 1) * HD, :] = out[:, g * tokens : (g + 1) * tokens]
    else:
        top_ref[...] = jnp.broadcast_to(top, top_ref.shape)
        norm_ref[...] = jnp.broadcast_to(norm, norm_ref.shape)
        acc_ref[...] = acc


def forward(q, pieces, carried, score_scale):
    tokens = q.shape[0]
    rows = GROUP * tokens
    half = sum(piece.shape[0] for piece in pieces)
    weights = jax.ShapeDtypeStruct((half, rows), F32)
    row = jax.ShapeDtypeStruct((8, rows), F32)
    if carried:
        shapes = (
            jax.ShapeDtypeStruct((GROUP * HD, tokens), F32),
            weights,
            jax.ShapeDtypeStruct((16, rows), F32),
        )
    else:
        shapes = row, row, jax.ShapeDtypeStruct((HD, rows), F32), weights
    return pl.pallas_call(
        functools.partial(forward_kernel, score_scale, 1 if carried else 0),
        out_shape=shapes,
        scratch_shapes=[
            pltpu.VMEM((half, HD), F32),
            pltpu.VMEM((half, HD), F32),
            pltpu.VMEM((half, rows), F32),
        ],
        compiler_params=params(12 * half * rows),
        cost_estimate=cost(36 * half * rows * HD, 8 * half * rows),
        name="attn_fwd",
    )(q, *pieces, *carried)


def stacked_queries(q_ref):
    return jnp.concatenate([q_ref[:, g * HD : (g + 1) * HD] for g in range(GROUP)], axis=0)


def stacked_grads(d_ref):
    return jnp.concatenate([d_ref[g * HD : (g + 1) * HD, :] for g in range(GROUP)], axis=1)


def key_grads(score_scale, q, d, exp_ref, inv, dp_ref, delta, keys, out_ref, acc):
    tokens = q.shape[0] // GROUP
    step = key_step(keys.shape[0], tokens)
    qh, ql = two(q)
    qhl = jnp.concatenate([qh, ql], axis=1)
    dh, dl = two(d)
    dhl = jnp.concatenate([dh, dl], axis=0)

    def grads(b, acc):
        at = pl.ds(pl.multiple_of(b * step, step), step)
        p = exp_ref[at, :] * inv
        ds = p * (dp_ref[at, :] - delta) * score_scale
        ph, plo = two(p)
        sh, sl = two(ds)
        kh, kl = two(keys[at, :].T)
        both = mm(jnp.concatenate([kh, kl], axis=0), sh)
        acc = acc + (both[:HD] + both[HD:] + mm(kh, sl))
        dk = mm(sh, qhl)
        out_ref[at, 0:HD] = dk[:, :HD] + dk[:, HD:] + mm(sl, qh)
        dv = mm(ph, dhl, NT)
        out_ref[at, HD : 2 * HD] = dv[:, :HD] + dv[:, HD:] + mm(plo, dh, NT)
        return acc

    return lax.fori_loop(0, keys.shape[0] // step, grads, acc)


def backward_far_kernel(score_scale, q_ref, d_ref, near_ref, far_ref, inv_ref, *refs):
    *pieces, acc_ref, dp_ref, delta_ref, send_ref, keys, values, far_dp = refs
    tokens = q_ref.shape[0]
    rows = GROUP * tokens
    half = keys.shape[0]
    step = key_step(half, tokens)
    load_blocks(pieces[-1:], keys, 0)
    load_blocks(pieces, values, HD)
    d = stacked_grads(d_ref)
    dh, dl = two(d)
    dhh = jnp.concatenate([dh, dh], axis=0)

    def probs(exp_ref, out_ref, first):
        def one(b, total):
            at = pl.ds(pl.multiple_of(b * step, step), step)
            vh, vl = two(values[pl.ds(pl.multiple_of(first + b * step, step), step), :])
            dp = mm(vh, dl) + mm(jnp.concatenate([vh, vl], axis=1), dhh)
            out_ref[at, :] = dp
            return total + jnp.sum(exp_ref[at, :] * dp, axis=0, keepdims=True)

        return lax.fori_loop(0, half // step, one, jnp.zeros((1, rows), F32))

    inv = inv_ref[8:9, :]
    delta = probs(near_ref, dp_ref, 0) * inv_ref[0:1, :] + probs(far_ref, far_dp, half) * inv
    delta_ref[...] = jnp.broadcast_to(delta, delta_ref.shape)
    acc_ref[...] = key_grads(
        score_scale,
        stacked_queries(q_ref),
        d,
        far_ref,
        inv,
        far_dp,
        delta,
        keys,
        send_ref,
        jnp.zeros((HD, rows), F32),
    )


def backward_near_kernel(
    score_scale, q_ref, d_ref, near_ref, inv_ref, acc_ref, dp_ref, delta_ref, *refs
):
    *pieces, dq_ref, keep_ref, keys = refs
    tokens = q_ref.shape[0]
    load_blocks(pieces, keys, 0)
    acc = key_grads(
        score_scale,
        stacked_queries(q_ref),
        stacked_grads(d_ref),
        near_ref,
        inv_ref[0:1, :],
        dp_ref,
        delta_ref[0:1, :],
        keys,
        keep_ref,
        acc_ref[...],
    )
    for g in range(GROUP):
        dq_ref[:, g * HD : (g + 1) * HD] = acc[:, g * tokens : (g + 1) * tokens].T


def backward_far(q, d_attn, near, far, inv, pieces, score_scale):
    half, rows = far.shape
    return pl.pallas_call(
        functools.partial(backward_far_kernel, score_scale),
        out_shape=(
            jax.ShapeDtypeStruct((HD, rows), F32),
            jax.ShapeDtypeStruct((half, rows), F32),
            jax.ShapeDtypeStruct((8, rows), F32),
            jax.ShapeDtypeStruct((half, 2 * HD), F32),
        ),
        scratch_shapes=[
            pltpu.VMEM((half, HD), F32),
            pltpu.VMEM((2 * half, HD), F32),
            pltpu.VMEM((half, rows), F32),
        ],
        compiler_params=params(24 * half * rows),
        cost_estimate=cost(48 * half * rows * HD, 16 * half * rows),
        name="attn_bwd_far",
    )(q, d_attn, near, far, inv, *pieces)


def backward_near(q, d_attn, near, inv, carried, pieces, score_scale):
    half, rows = near.shape
    return pl.pallas_call(
        functools.partial(backward_near_kernel, score_scale),
        out_shape=(
            jax.ShapeDtypeStruct(q.shape, F32),
            jax.ShapeDtypeStruct((half, 2 * HD), F32),
        ),
        scratch_shapes=[pltpu.VMEM((half, HD), F32)],
        compiler_params=params(12 * half * rows),
        cost_estimate=cost(36 * half * rows * HD, 8 * half * rows),
        name="attn_bwd_near",
    )(q, d_attn, near, inv, *carried, *pieces)


def project_kernel(new, old, side, width, *refs):
    refs = list(refs)

    def take(count):
        taken = refs[:count]
        del refs[:count]
        return taken

    (w_ref,) = take(1)
    fresh = [[take(n) for n in counts] for _, counts in new]
    stale = [[take(n) for n in counts] for _, counts in old] if side else []
    carried = take(1) if old else []
    (d_ref,) = take(1)
    outs = take(len(column_sets(side))) if side else []
    weights, sem = (w_ref, None) if old else take(2)
    heads, rows, part = weights.shape
    tokens = d_ref.shape[1]
    me = lax.axis_index("head")

    def block(copies):
        whole = [
            jnp.concatenate([ref[...] for ref in rows], axis=0) if len(rows) > 1 else rows[0][...]
            for rows in copies
        ]
        return functools.reduce(jnp.add, whole)

    def column(offset):
        return pl.ds(pl.multiple_of((me ^ offset) * part, part), part)

    copies = {}
    if not old:
        for d in range(heads):
            copies[d] = pltpu.make_async_copy(w_ref.at[:, column(d)], weights.at[d], sem.at[d])
            copies[d].start()
    if side:
        (full,) = take(1)
        for piece, offset in zip(stale + fresh, [o for o, _ in old + new]):
            full[:, column(offset)] = block(piece)
        seq = lax.axis_index("seq")
        core = seq % CORES
        chip = seq // CORES
        x, y = chip % side, chip // side
        for out, (other_core, j) in zip(outs, column_sets(side)):
            kind = core ^ other_core
            fixed = jnp.where(kind == 0, x, y) ^ j
            moving = jnp.where(kind == 0, y, x)
            for t in range(side):
                i = moving ^ t
                index = jnp.where(kind == 0, i * side + fixed, fixed * side + i)
                at = pl.multiple_of((index * CORES + kind) * width, width)
                out[:, t * width : (t + 1) * width] = full[:, pl.ds(at, width)]
    step = rows // 2
    for i, (piece, (d, _)) in enumerate(zip(fresh, new)):
        g_hi, g_lo = two(block(piece))
        g_both = jnp.concatenate([g_hi, g_lo], axis=0)
        if d in copies:
            copies.pop(d).wait()
        for row in range(0, rows, step):
            at = slice(row, row + step)
            w_hi, w_lo = two(weights[d, at, :])
            both = mm(w_hi, g_both, NT)
            value = both[:, :tokens] + both[:, tokens:] + mm(w_lo, g_hi, NT)
            if i or carried:
                value = value + (d_ref if i else carried[0])[at, :]
            d_ref[at, :] = value
    for copy in copies.values():
        copy.wait()


def column_sets(side):
    sets = [(0, 0)]
    for j in range(side):
        if j:
            sets.append((0, j))
        sets.append((1, j))
    return sets


def project(weight, blocks, new, old, carried, side, width):
    heads = lax.axis_size("head")
    tokens = sum(piece.shape[0] for piece in blocks[0][0])
    if old:
        _, rows, part = weight.shape
    else:
        rows, part = weight.shape[0], weight.shape[1] // heads
    shapes = [jax.ShapeDtypeStruct((rows, tokens), F32)]
    scratch = []
    operands = [piece for d in new for copy in blocks[d] for piece in copy]
    if side:
        shapes += [jax.ShapeDtypeStruct((tokens, side * width), F32)] * len(column_sets(side))
        scratch.append(pltpu.VMEM((tokens, heads * part), F32))
        operands += [piece for d in old for copy in blocks[d] for piece in copy]
    if old:
        operands.append(carried)
    else:
        weight = in_hbm(weight)
        shapes.append(jax.ShapeDtypeStruct((heads, rows, part), F32))
        scratch.append(pltpu.SemaphoreType.DMA((heads,)))

    def counted(distances):
        return [(d, tuple(len(copy) for copy in blocks[d])) for d in distances]

    return pl.pallas_call(
        functools.partial(project_kernel, counted(new), counted(old), side, width),
        out_shape=tuple(shapes),
        in_specs=[pl.BlockSpec(memory_space=pltpu.VMEM if old else pltpu.HBM)]
        + [pl.BlockSpec(memory_space=pltpu.VMEM)] * len(operands),
        scratch_shapes=scratch,
        compiler_params=params(8 * heads * rows * part),
        cost_estimate=cost(24 * tokens * rows * part * len(new), 4 * rows * part * len(new)),
        name="project",
    )(weight, *operands)


def weight_kernel(first, count, *refs):
    attn = refs[:count]
    grad = refs[count : 2 * count]
    outs = refs[2 * count :]
    width = outs[0].shape[1]
    a_hi, a_lo = two(jnp.concatenate([ref[...] for ref in attn], axis=1))
    for t, out in enumerate(outs, first):
        cut = slice(t * width, (t + 1) * width)
        g_hi, g_lo = two(jnp.concatenate([ref[:, cut] for ref in grad], axis=0))
        out[...] = mm(a_hi, g_lo) + mm(a_lo, g_hi) + mm(a_hi, g_hi)


def weight_grad(attn, grad, first, last, width):
    rows = attn[0].shape[0]
    outs = last - first
    return pl.pallas_call(
        functools.partial(weight_kernel, first, len(attn)),
        out_shape=(jax.ShapeDtypeStruct((rows, width), F32),) * outs,
        compiler_params=params(),
        cost_estimate=cost(6 * rows * rows * width * outs, 8 * rows * width * outs),
        name="weight_grad",
    )(*attn, *grad)


def body(queries, keys, values, grad_out, out_weight):
    tokens = queries.shape[0]
    seq = lax.axis_size("seq")
    heads = lax.axis_size("head")
    chips = seq // CORES
    width = out_weight.shape[1] // seq
    score_scale = 1.0 / math.sqrt(HD)
    side = math.isqrt(chips)
    exchange = side * side == chips and width % 128 == 0

    def swap(block):
        return lax.ppermute(block, "seq", [(i, i ^ 1) for i in range(seq)])

    def to_chip(block, j):
        return lax.ppermute(block, "seq", [(i, i ^ (CORES * j)) for i in range(seq)])

    def along(block, route):
        return lax.ppermute(block, "head", route)

    own, upper, lower = pack(keys, values, grad_out)
    by_distance = {0: ((upper, lower),)}
    for d in range(1, heads):
        pairs = [(i, i ^ d) for i in range(heads)]
        if heads != GROUP or d == 1:
            by_distance[d] = ((along(grad_out, pairs),),)
        elif d == 2:
            by_distance[d] = ((along(upper, pairs), along(lower, pairs)),)
        else:
            ends = [(1, 0), (2, 3)]
            ((near_upper, near_lower),) = by_distance[2]
            by_distance[d] = (
                (along(grad_out, [(1, 2), (2, 1)]),),
                (along(near_upper, ends), along(near_lower, ends)),
            )

    same = [own]
    for j in range(1, chips):
        same.append(to_chip(own, j))
    pieces = same + [swap(jnp.concatenate(same, axis=0))]

    *carried, near = forward(queries, same, (), score_scale)
    attn, far, inv = forward(queries, pieces[-1:], carried, score_scale)
    weight, d_attn, column = out_weight, None, ()
    seen = []
    for fresh in ([0], [1], list(range(2, heads))):
        final = fresh[-1] == heads - 1
        d_attn, *column = project(
            weight, by_distance, fresh, seen, d_attn, side if exchange and final else 0, width
        )
        if not seen:
            weight = column.pop()
        seen = seen + fresh
        if final:
            break

    if exchange:

        def routes(cross, j):
            found = []
            for i in range(seq):
                core, chip = i % CORES, i // CORES
                kind = core ^ cross
                x, y = chip % side, chip // side
                if kind == 0:
                    x ^= j
                else:
                    y ^= j
                found.append((i, (y * side + x) * CORES + kind))
            return found

        sets = column_sets(side)
        moved_grad, moved_attn = [column[0]], [attn]
        for i in range(1, len(sets)):
            moved_attn.append(lax.ppermute(attn, "seq", routes(*sets[i])))
            moved_grad.append(lax.ppermute(column[i], "seq", routes(*sets[i])))
        partial = weight_grad(moved_attn, moved_grad, 1, side, width)

        def final_routes(t):
            found = []
            for i in range(seq):
                core, chip = i % CORES, i // CORES
                x, y = chip % side, chip // side
                if core == 0:
                    y ^= t
                else:
                    x ^= t
                found.append((i, (y * side + x) * CORES + core))
            return found

        arrived = []
        for t in range(1, side):
            arrived.append(lax.ppermute(partial[t - 1], "seq", final_routes(t)))
        (grad_wo,) = weight_grad(moved_attn, moved_grad, 0, 1, width)
        for moved in arrived:
            grad_wo = grad_wo + moved
    else:
        grad_full = lax.all_gather(grad_out, "head", axis=1, tiled=True)
        grad_wo = lax.psum_scatter(
            jnp.dot(grad_full.T, attn.T, precision=lax.Precision.HIGHEST),
            "seq",
            scatter_dimension=0,
            tiled=True,
        ).T

    *carried, send = backward_far(queries, d_attn, near, far, inv, pieces, score_scale)
    swapped = swap(send)
    grad_q, keep = backward_near(queries, d_attn, near, inv, carried, same, score_scale)
    summed = (keep + swapped).reshape(chips, tokens, 2 * HD)
    grad_kv = summed[0]
    for j in range(1, chips):
        moved = to_chip(summed[j], j)
        grad_kv = grad_kv + moved
    return (grad_q, grad_kv[:, :HD], grad_kv[:, HD:], grad_wo)


def solution(mesh):
    in_specs = (
        P("seq", "head"),
        P("seq", "head"),
        P("seq", "head"),
        P("seq", "head"),
        P("head", None),
    )
    out_specs = (P("seq", "head"), P("seq", "head"), P("seq", "head"), P("head", "seq"))
    return jax.shard_map(
        body,
        mesh=mesh,
        in_specs=in_specs,
        out_specs=out_specs,
        check_vma=False,
    )
```

```python
import functools
import math

import jax
import jax.numpy as jnp
from jax import lax
from jax.experimental import pallas as pl
from jax.experimental.pallas import tpu as pltpu
from jax.sharding import PartitionSpec as P

HD = 128
GROUP = 4
CORES = 2
MASKED = -1e30
STEP = 4
FIRST = 6
F32 = jnp.float32
BF16 = jnp.bfloat16

NN = (((1,), (0,)), ((), ()))
NT = (((1,), (1,)), ((), ()))


def mm(a, b, dims=NN):
    return lax.dot_general(a, b, dims, preferred_element_type=F32)


def two(x):
    hi = x.astype(BF16)
    return hi, (x - hi.astype(F32)).astype(BF16)


def three(x):
    first = x.astype(BF16)
    rest = x - first.astype(F32)
    second = rest.astype(BF16)
    return first, second, (rest - second.astype(F32)).astype(BF16)


def cost(flops, size):
    return pl.CostEstimate(flops=flops, transcendentals=0, bytes_accessed=size)


def params(held=0):
    return pltpu.CompilerParams(vmem_limit_bytes=(12 << 20) + held)


def in_hbm(x):
    return pltpu.with_memory_space_constraint(x, pltpu.HBM)


def key_step(count, tokens):
    return next(tokens * n for n in (STEP, 2, 1) if count % (tokens * n) == 0)


def load_blocks(refs, dst, column):
    row = 0
    for ref in refs:
        count = ref.shape[0]
        dst[row : row + count, :] = ref[:, column : column + HD]
        row += count


def first_part(tokens):
    return tokens * FIRST // 8


def pack_kernel(keys_ref, values_ref, grad_ref, out_ref, upper_ref, lower_ref, sem):
    count = upper_ref.shape[0]
    pairs = (
        (keys_ref, out_ref.at[:, :HD]),
        (values_ref, out_ref.at[:, HD:]),
        (grad_ref.at[:count], upper_ref),
        (grad_ref.at[count:], lower_ref),
    )
    copies = [pltpu.make_async_copy(a, b, sem.at[i]) for i, (a, b) in enumerate(pairs)]
    for copy in copies:
        copy.start()
    for copy in copies:
        copy.wait()


def pack(keys, values, grad_out):
    tokens, columns = grad_out.shape
    upper = first_part(tokens)
    parts = [jax.ShapeDtypeStruct((n, columns), F32) for n in (upper, tokens - upper)]
    return pl.pallas_call(
        pack_kernel,
        out_shape=(jax.ShapeDtypeStruct((tokens, 2 * HD), F32), *parts),
        in_specs=[pl.BlockSpec(memory_space=pltpu.HBM)] * 3,
        scratch_shapes=[pltpu.SemaphoreType.DMA((4,))],
        compiler_params=params(),
        name="pack",
    )(*(in_hbm(x) for x in (keys, values, grad_out)))


def forward_kernel(score_scale, other, q_ref, *refs):
    if other:
        *pieces, top_ref, norm_ref, acc_ref, attn_ref, exp_ref, inv_ref, keys, values, score = refs
    else:
        *pieces, top_ref, norm_ref, acc_ref, exp_ref, keys, values, score = refs
    tokens = q_ref.shape[0]
    rows = GROUP * tokens
    step = key_step(keys.shape[0], tokens)
    steps = keys.shape[0] // step
    me = lax.axis_index("seq")
    load_blocks(pieces, keys, 0)
    load_blocks(pieces, values, HD)
    q1, q2, q3 = three(stacked_queries(q_ref))
    q11 = jnp.concatenate([q1, q1], axis=1)
    q22 = jnp.concatenate([q2, q2], axis=1)
    q13 = jnp.concatenate([q1, q3], axis=1)
    key_row = lax.broadcasted_iota(jnp.int32, (tokens, rows), 0)
    query_row = lax.broadcasted_iota(jnp.int32, (tokens, rows), 1) % tokens
    offset = key_row - query_row

    def scores(b, top):
        k1, k2, k3 = three(keys[pl.ds(pl.multiple_of(b * step, step), step), :])
        k12 = jnp.concatenate([k1, k2], axis=1)
        k31 = jnp.concatenate([k3, k1], axis=1)
        found = mm(k31, q13, NT) + mm(k12, q22, NT) + mm(k12, q11, NT)
        for i in range(step // tokens):
            which = b * (step // tokens) + i
            block = ((me // CORES) ^ which) * CORES + ((me % CORES) ^ other)
            s = found[i * tokens : (i + 1) * tokens] * score_scale
            s = jnp.where(offset <= (me - block) * tokens, s, MASKED)
            score[pl.ds(pl.multiple_of(which * tokens, tokens), tokens), :] = s
            top = jnp.maximum(top, jnp.max(s, axis=0, keepdims=True))
        return top

    before = top_ref[0:1, :] if other else jnp.full((1, rows), MASKED, F32)
    top = lax.fori_loop(0, steps, scores, before)

    def weigh(b, state):
        norm, acc = state
        at = pl.ds(pl.multiple_of(b * step, step), step)
        e = jnp.exp(score[at, :] - top)
        exp_ref[at, :] = e
        eh, el = two(e)
        vh, vl = two(values[at, :].T)
        both = mm(jnp.concatenate([vh, vl], axis=0), eh)
        acc = acc + (both[:HD] + both[HD:] + mm(vh, el))
        return norm + jnp.sum(e, axis=0, keepdims=True), acc

    if other:
        factor = jnp.exp(before - top)
        start = norm_ref[0:1, :] * factor, acc_ref[...] * factor
    else:
        start = jnp.zeros((1, rows), F32), jnp.zeros((HD, rows), F32)
    norm, acc = lax.fori_loop(0, steps, weigh, start)
    if other:
        inv = 1.0 / norm
        inv_ref[0:8, :] = jnp.broadcast_to(inv * factor, (8, rows))
        inv_ref[8:16, :] = jnp.broadcast_to(inv, (8, rows))
        out = acc * inv
        for g in range(GROUP):
            attn_ref[g * HD : (g + 1) * HD, :] = out[:, g * tokens : (g + 1) * tokens]
    else:
        top_ref[...] = jnp.broadcast_to(top, top_ref.shape)
        norm_ref[...] = jnp.broadcast_to(norm, norm_ref.shape)
        acc_ref[...] = acc


def forward(q, pieces, carried, score_scale):
    tokens = q.shape[0]
    rows = GROUP * tokens
    half = sum(piece.shape[0] for piece in pieces)
    weights = jax.ShapeDtypeStruct((half, rows), F32)
    row = jax.ShapeDtypeStruct((8, rows), F32)
    if carried:
        shapes = (
            jax.ShapeDtypeStruct((GROUP * HD, tokens), F32),
            weights,
            jax.ShapeDtypeStruct((16, rows), F32),
        )
    else:
        shapes = row, row, jax.ShapeDtypeStruct((HD, rows), F32), weights
    return pl.pallas_call(
        functools.partial(forward_kernel, score_scale, 1 if carried else 0),
        out_shape=shapes,
        scratch_shapes=[
            pltpu.VMEM((half, HD), F32),
            pltpu.VMEM((half, HD), F32),
            pltpu.VMEM((half, rows), F32),
        ],
        compiler_params=params(12 * half * rows),
        cost_estimate=cost(36 * half * rows * HD, 8 * half * rows),
        name="attn_fwd",
    )(q, *pieces, *carried)


def stacked_queries(q_ref):
    return jnp.concatenate([q_ref[:, g * HD : (g + 1) * HD] for g in range(GROUP)], axis=0)


def stacked_grads(d_ref):
    return jnp.concatenate([d_ref[g * HD : (g + 1) * HD, :] for g in range(GROUP)], axis=1)


def key_grads(score_scale, q, d, exp_ref, inv, dp_ref, delta, keys, out_ref, acc):
    tokens = q.shape[0] // GROUP
    step = key_step(keys.shape[0], tokens)
    qh, ql = two(q)
    qhl = jnp.concatenate([qh, ql], axis=1)
    dh, dl = two(d)
    dhl = jnp.concatenate([dh, dl], axis=0)

    def grads(b, acc):
        at = pl.ds(pl.multiple_of(b * step, step), step)
        p = exp_ref[at, :] * inv
        ds = p * (dp_ref[at, :] - delta) * score_scale
        ph, plo = two(p)
        sh, sl = two(ds)
        kh, kl = two(keys[at, :].T)
        both = mm(jnp.concatenate([kh, kl], axis=0), sh)
        acc = acc + (both[:HD] + both[HD:] + mm(kh, sl))
        dk = mm(sh, qhl)
        out_ref[at, 0:HD] = dk[:, :HD] + dk[:, HD:] + mm(sl, qh)
        dv = mm(ph, dhl, NT)
        out_ref[at, HD : 2 * HD] = dv[:, :HD] + dv[:, HD:] + mm(plo, dh, NT)
        return acc

    return lax.fori_loop(0, keys.shape[0] // step, grads, acc)


def backward_far_kernel(score_scale, q_ref, d_ref, near_ref, far_ref, inv_ref, *refs):
    *pieces, acc_ref, dp_ref, delta_ref, send_ref, keys, values, far_dp = refs
    tokens = q_ref.shape[0]
    rows = GROUP * tokens
    half = keys.shape[0]
    step = key_step(half, tokens)
    load_blocks(pieces[-1:], keys, 0)
    load_blocks(pieces, values, HD)
    d = stacked_grads(d_ref)
    dh, dl = two(d)
    dhh = jnp.concatenate([dh, dh], axis=0)

    def probs(exp_ref, out_ref, first):
        def one(b, total):
            at = pl.ds(pl.multiple_of(b * step, step), step)
            vh, vl = two(values[pl.ds(pl.multiple_of(first + b * step, step), step), :])
            dp = mm(vh, dl) + mm(jnp.concatenate([vh, vl], axis=1), dhh)
            out_ref[at, :] = dp
            return total + jnp.sum(exp_ref[at, :] * dp, axis=0, keepdims=True)

        return lax.fori_loop(0, half // step, one, jnp.zeros((1, rows), F32))

    inv = inv_ref[8:9, :]
    delta = probs(near_ref, dp_ref, 0) * inv_ref[0:1, :] + probs(far_ref, far_dp, half) * inv
    delta_ref[...] = jnp.broadcast_to(delta, delta_ref.shape)
    acc_ref[...] = key_grads(
        score_scale,
        stacked_queries(q_ref),
        d,
        far_ref,
        inv,
        far_dp,
        delta,
        keys,
        send_ref,
        jnp.zeros((HD, rows), F32),
    )


def backward_near_kernel(
    score_scale, q_ref, d_ref, near_ref, inv_ref, acc_ref, dp_ref, delta_ref, *refs
):
    *pieces, dq_ref, keep_ref, keys = refs
    tokens = q_ref.shape[0]
    load_blocks(pieces, keys, 0)
    acc = key_grads(
        score_scale,
        stacked_queries(q_ref),
        stacked_grads(d_ref),
        near_ref,
        inv_ref[0:1, :],
        dp_ref,
        delta_ref[0:1, :],
        keys,
        keep_ref,
        acc_ref[...],
    )
    for g in range(GROUP):
        dq_ref[:, g * HD : (g + 1) * HD] = acc[:, g * tokens : (g + 1) * tokens].T


def backward_far(q, d_attn, near, far, inv, pieces, score_scale):
    half, rows = far.shape
    return pl.pallas_call(
        functools.partial(backward_far_kernel, score_scale),
        out_shape=(
            jax.ShapeDtypeStruct((HD, rows), F32),
            jax.ShapeDtypeStruct((half, rows), F32),
            jax.ShapeDtypeStruct((8, rows), F32),
            jax.ShapeDtypeStruct((half, 2 * HD), F32),
        ),
        scratch_shapes=[
            pltpu.VMEM((half, HD), F32),
            pltpu.VMEM((2 * half, HD), F32),
            pltpu.VMEM((half, rows), F32),
        ],
        compiler_params=params(24 * half * rows),
        cost_estimate=cost(48 * half * rows * HD, 16 * half * rows),
        name="attn_bwd_far",
    )(q, d_attn, near, far, inv, *pieces)


def backward_near(q, d_attn, near, inv, carried, pieces, score_scale):
    half, rows = near.shape
    return pl.pallas_call(
        functools.partial(backward_near_kernel, score_scale),
        out_shape=(
            jax.ShapeDtypeStruct(q.shape, F32),
            jax.ShapeDtypeStruct((half, 2 * HD), F32),
        ),
        scratch_shapes=[pltpu.VMEM((half, HD), F32)],
        compiler_params=params(12 * half * rows),
        cost_estimate=cost(36 * half * rows * HD, 8 * half * rows),
        name="attn_bwd_near",
    )(q, d_attn, near, inv, *carried, *pieces)


def project_kernel(new, old, side, width, *refs):
    refs = list(refs)

    def take(count):
        taken = refs[:count]
        del refs[:count]
        return taken

    (w_ref,) = take(1)
    fresh = [[take(n) for n in counts] for _, counts in new]
    stale = [[take(n) for n in counts] for _, counts in old] if side else []
    carried = take(1) if old else []
    (d_ref,) = take(1)
    outs = take(len(column_sets(side))) if side else []
    weights, sem = (w_ref, None) if old else take(2)
    heads, rows, part = weights.shape
    tokens = d_ref.shape[1]
    me = lax.axis_index("head")

    def block(copies):
        whole = [
            jnp.concatenate([ref[...] for ref in rows], axis=0) if len(rows) > 1 else rows[0][...]
            for rows in copies
        ]
        return functools.reduce(jnp.add, whole)

    def column(offset):
        return pl.ds(pl.multiple_of((me ^ offset) * part, part), part)

    copies = {}
    if not old:
        for d in range(heads):
            copies[d] = pltpu.make_async_copy(w_ref.at[:, column(d)], weights.at[d], sem.at[d])
            copies[d].start()
    if side:
        (full,) = take(1)
        for piece, offset in zip(stale + fresh, [o for o, _ in old + new]):
            full[:, column(offset)] = block(piece)
        seq = lax.axis_index("seq")
        core = seq % CORES
        chip = seq // CORES
        x, y = chip % side, chip // side
        for out, (other_core, j) in zip(outs, column_sets(side)):
            kind = core ^ other_core
            fixed = jnp.where(kind == 0, x, y) ^ j
            moving = jnp.where(kind == 0, y, x)
            for t in range(side):
                i = moving ^ t
                index = jnp.where(kind == 0, i * side + fixed, fixed * side + i)
                at = pl.multiple_of((index * CORES + kind) * width, width)
                out[:, t * width : (t + 1) * width] = full[:, pl.ds(at, width)]
    step = rows // 2
    for i, (piece, (d, _)) in enumerate(zip(fresh, new)):
        g_hi, g_lo = two(block(piece))
        g_both = jnp.concatenate([g_hi, g_lo], axis=0)
        if d in copies:
            copies.pop(d).wait()
        for row in range(0, rows, step):
            at = slice(row, row + step)
            w_hi, w_lo = two(weights[d, at, :])
            both = mm(w_hi, g_both, NT)
            value = both[:, :tokens] + both[:, tokens:] + mm(w_lo, g_hi, NT)
            if i or carried:
                value = value + (d_ref if i else carried[0])[at, :]
            d_ref[at, :] = value
    for copy in copies.values():
        copy.wait()


def column_sets(side):
    sets = [(0, 0)]
    for j in range(side):
        if j:
            sets.append((0, j))
        sets.append((1, j))
    return sets


def project(weight, blocks, new, old, carried, side, width):
    heads = lax.axis_size("head")
    tokens = sum(piece.shape[0] for piece in blocks[0][0])
    if old:
        _, rows, part = weight.shape
    else:
        rows, part = weight.shape[0], weight.shape[1] // heads
    shapes = [jax.ShapeDtypeStruct((rows, tokens), F32)]
    scratch = []
    operands = [piece for d in new for copy in blocks[d] for piece in copy]
    if side:
        shapes += [jax.ShapeDtypeStruct((tokens, side * width), F32)] * len(column_sets(side))
        scratch.append(pltpu.VMEM((tokens, heads * part), F32))
        operands += [piece for d in old for copy in blocks[d] for piece in copy]
    if old:
        operands.append(carried)
    else:
        weight = in_hbm(weight)
        shapes.append(jax.ShapeDtypeStruct((heads, rows, part), F32))
        scratch.append(pltpu.SemaphoreType.DMA((heads,)))

    def counted(distances):
        return [(d, tuple(len(copy) for copy in blocks[d])) for d in distances]

    return pl.pallas_call(
        functools.partial(project_kernel, counted(new), counted(old), side, width),
        out_shape=tuple(shapes),
        in_specs=[pl.BlockSpec(memory_space=pltpu.VMEM if old else pltpu.HBM)]
        + [pl.BlockSpec(memory_space=pltpu.VMEM)] * len(operands),
        scratch_shapes=scratch,
        compiler_params=params(8 * heads * rows * part),
        cost_estimate=cost(24 * tokens * rows * part * len(new), 4 * rows * part * len(new)),
        name="project",
    )(weight, *operands)


def weight_kernel(first, count, *refs):
    attn = refs[:count]
    grad = refs[count : 2 * count]
    outs = refs[2 * count :]
    width = outs[0].shape[1]
    a_hi, a_lo = two(jnp.concatenate([ref[...] for ref in attn], axis=1))
    for t, out in enumerate(outs, first):
        cut = slice(t * width, (t + 1) * width)
        g_hi, g_lo = two(jnp.concatenate([ref[:, cut] for ref in grad], axis=0))
        out[...] = mm(a_hi, g_lo) + mm(a_lo, g_hi) + mm(a_hi, g_hi)


def weight_grad(attn, grad, first, last, width):
    rows = attn[0].shape[0]
    outs = last - first
    return pl.pallas_call(
        functools.partial(weight_kernel, first, len(attn)),
        out_shape=(jax.ShapeDtypeStruct((rows, width), F32),) * outs,
        compiler_params=params(),
        cost_estimate=cost(6 * rows * rows * width * outs, 8 * rows * width * outs),
        name="weight_grad",
    )(*attn, *grad)


def body(queries, keys, values, grad_out, out_weight):
    tokens = queries.shape[0]
    seq = lax.axis_size("seq")
    heads = lax.axis_size("head")
    chips = seq // CORES
    width = out_weight.shape[1] // seq
    score_scale = 1.0 / math.sqrt(HD)
    side = math.isqrt(chips)
    exchange = side * side == chips and width % 128 == 0

    def swap(block):
        return lax.ppermute(block, "seq", [(i, i ^ 1) for i in range(seq)])

    def to_chip(block, j):
        return lax.ppermute(block, "seq", [(i, i ^ (CORES * j)) for i in range(seq)])

    def along(block, route):
        return lax.ppermute(block, "head", route)

    own, upper, lower = pack(keys, values, grad_out)
    by_distance = {0: ((upper, lower),)}
    for d in range(1, heads):
        pairs = [(i, i ^ d) for i in range(heads)]
        if heads != GROUP or d == 1:
            by_distance[d] = ((along(grad_out, pairs),),)
        elif d == 2:
            by_distance[d] = ((along(upper, pairs), along(lower, pairs)),)
        else:
            ends = [(1, 0), (2, 3)]
            ((near_upper, near_lower),) = by_distance[2]
            by_distance[d] = (
                (along(grad_out, [(1, 2), (2, 1)]),),
                (along(near_upper, ends), along(near_lower, ends)),
            )

    same = [own]
    for j in range(1, chips):
        same.append(to_chip(own, j))
    pieces = same + [swap(jnp.concatenate(same, axis=0))]

    *carried, near = forward(queries, same, (), score_scale)
    attn, far, inv = forward(queries, pieces[-1:], carried, score_scale)
    weight, d_attn, column = out_weight, None, ()
    seen = []
    for fresh in ([0], [1], list(range(2, heads))):
        final = fresh[-1] == heads - 1
        d_attn, *column = project(
            weight, by_distance, fresh, seen, d_attn, side if exchange and final else 0, width
        )
        if not seen:
            weight = column.pop()
        seen = seen + fresh
        if final:
            break

    if exchange:

        def routes(cross, j):
            found = []
            for i in range(seq):
                core, chip = i % CORES, i // CORES
                kind = core ^ cross
                x, y = chip % side, chip // side
                if kind == 0:
                    x ^= j
                else:
                    y ^= j
                found.append((i, (y * side + x) * CORES + kind))
            return found

        sets = column_sets(side)
        moved_grad, moved_attn = [column[0]], [attn]
        for i in range(1, len(sets)):
            moved_attn.append(lax.ppermute(attn, "seq", routes(*sets[i])))
            moved_grad.append(lax.ppermute(column[i], "seq", routes(*sets[i])))
        partial = weight_grad(moved_attn, moved_grad, 1, side, width)

        def final_routes(t):
            found = []
            for i in range(seq):
                core, chip = i % CORES, i // CORES
                x, y = chip % side, chip // side
                if core == 0:
                    y ^= t
                else:
                    x ^= t
                found.append((i, (y * side + x) * CORES + core))
            return found

        arrived = []
        for t in range(1, side):
            arrived.append(lax.ppermute(partial[t - 1], "seq", final_routes(t)))
        (grad_wo,) = weight_grad(moved_attn, moved_grad, 0, 1, width)
        for moved in arrived:
            grad_wo = grad_wo + moved
    else:
        grad_full = lax.all_gather(grad_out, "head", axis=1, tiled=True)
        grad_wo = lax.psum_scatter(
            jnp.dot(grad_full.T, attn.T, precision=lax.Precision.HIGHEST),
            "seq",
            scatter_dimension=0,
            tiled=True,
        ).T

    *carried, send = backward_far(queries, d_attn, near, far, inv, pieces, score_scale)
    swapped = swap(send)
    grad_q, keep = backward_near(queries, d_attn, near, inv, carried, same, score_scale)
    summed = (keep + swapped).reshape(chips, tokens, 2 * HD)
    grad_kv = summed[0]
    for j in range(1, chips):
        moved = to_chip(summed[j], j)
        grad_kv = grad_kv + moved
    return (grad_q, grad_kv[:, :HD], grad_kv[:, HD:], grad_wo)


def solution(mesh):
    in_specs = (
        P("seq", "head"),
        P("seq", "head"),
        P("seq", "head"),
        P("seq", "head"),
        P("head", None),
    )
    out_specs = (P("seq", "head"), P("seq", "head"), P("seq", "head"), P("head", "seq"))
    return jax.shard_map(
        body,
        mesh=mesh,
        in_specs=in_specs,
        out_specs=out_specs,
        check_vma=False,
    )
```
